256 devices in a mesh: dp: 128 (over y, z, x), mp: 2 (over core).
Axes of the slice: x: 4, y: 4, z: 8, core: 2. Of those that a mesh axis runs over, the one named last changes fastest.
Arguments:
- features: bfloat16 [32768, 768], P('dp', 'mp'), may hold values from -0.21875 to 0.21875
- labels: int32 [32768], P('dp'), may hold values from 0 to 131071, as said below
- queries: bfloat16 [32768, 768], P('dp', 'mp'), may hold values from -240 to 240
- bank: float32 [131072, 768], P('dp', 'mp'), may hold values from -0.21875 to 0.21875
- old_conc: float32 [131072], P('dp'), may hold values from 0.4 to 0.6
- neg_index: int32 [8192], replicated, may hold values from 0 to 131071, as said below
Outputs:
- new_bank: float32 [131072, 768], P('dp', 'mp')
- new_conc: float32 [131072], P('dp')
- loss: float32 [32768], P('dp')
- grad: float32 [32768, 768], P('dp', 'mp')
The draws below stay inside these ranges and needn't reach their ends.
Inputs may be any that keep to these rules, and one draw needn't show every extreme that they name: In each aligned block of 256 rows, at most 6 labels fall in any one range of 1024 consecutive prototypes starting at a multiple of 1024; one such range receives exactly 6 labels from every block. `neg_index`: entries j * 64 to (j + 1) * 64 - 1 are distinct prototypes of the range j * 1024 to (j + 1) * 1024 - 1.
All inputs are finite; a program needn't handle non-finite values.
Results may differ from the reference program's by a relative error of at most 0.0074.
Values may be sent and summed in bfloat16 or wider, within the bound.
A program may use at most 64 MiB of HBM per device.

```python
import math
import jax
import jax.numpy as jnp
from jax import lax

D = 768
PROTO_DEV = 1024
FEAT_DEV = 256
NEG_DEV = 64
CAP = 6
PROTOS = 131072
FEATS = 32768
N_DP = 128


def draw_labels(key, part):
    slot_total = N_DP * CAP
    slot_owner = jnp.arange(slot_total, dtype=jnp.int32) // CAP
    hottest = jax.random.randint(jax.random.fold_in(key, 7), (), 0, N_DP)
    heavy = jax.random.permutation(jax.random.fold_in(key, 8), N_DP) < max(N_DP // 8, 1)
    factor = jnp.where(heavy[slot_owner], 4, 1)

    def one_block(block_key):
        key_score, key_order, key_local = jax.random.split(block_key, 3)
        score = jax.random.randint(key_score, (slot_total,), 0, 2 ** 16) * factor
        score = score * slot_total + jnp.arange(slot_total, dtype=jnp.int32)
        score = jnp.where(slot_owner == hottest, -1, score)
        chosen = lax.top_k(score, FEAT_DEV - CAP)[1]
        owners = jnp.concatenate([jnp.full((CAP,), hottest, jnp.int32), slot_owner[chosen]])
        owners = jax.random.permutation(key_order, owners)
        local = jax.random.randint(key_local, (FEAT_DEV,), 0, PROTO_DEV)
        return owners * PROTO_DEV + local
    keys = jax.random.split(jax.random.fold_in(key, 9), N_DP)
    return jax.vmap(one_block)(keys).reshape(-1).astype(jnp.int32)


def draw_neg_index(key, part):
    score = jax.random.randint(jax.random.fold_in(key, 11), (N_DP, PROTO_DEV), 0, 2 ** 16)
    score = score * PROTO_DEV + jnp.arange(PROTO_DEV, dtype=jnp.int32)[None, :]
    local = lax.top_k(score, NEG_DEV)[1]
    owners = jnp.arange(N_DP, dtype=jnp.int32)[:, None]
    return (owners * PROTO_DEV + local).reshape(-1).astype(jnp.int32)


def draw_queries(key, part):
    rows_all = FEAT_DEV * N_DP
    key_base = jax.random.fold_in(key, 21)
    key_rows = jax.random.fold_in(key, 22)
    base = jnp.clip(jax.random.normal(key_base, (rows_all, D), jnp.float32), -6.0, 6.0)
    boosted = jax.random.randint(key_rows, (rows_all,), 0, 32) == 0
    scale = jnp.where(boosted, 40.0, 1.0)
    return (base * scale[:, None]).astype(jnp.bfloat16)


def levels(rng, dims, shards, low, high):
    def one(position, blocks):
        heights = jax.random.uniform(jax.random.fold_in(jax.random.fold_in(rng, 6), position), (blocks,), jnp.float32, low / len(shards), high / len(shards))
        return jnp.repeat(jnp.exp(heights), dims[position] // blocks).reshape((-1,) + (1,) * (len(dims) - position - 1))

    level = one(*shards[0])
    for cut in shards[1:]:
        level = level * one(*cut)
    return level


def centred(own_key, dims, spread, limit, pieces=(), held_as=jnp.bfloat16):
    drawn = spread * jax.random.normal(own_key, dims, jnp.float32)
    if pieces:
        drawn = drawn * levels(own_key, dims, pieces, -0.22, 0.18)
    return jnp.clip(drawn, -limit, limit).astype(held_as)


def setup_inputs(seed: int = 0) -> dict:
    arg_keys = jax.random.split(jax.random.key(seed), 7)
    return {
        "features": centred(arg_keys[0], (FEATS, D), D ** -0.5, 0.21875, ((0, 128), (1, 2))),
        "labels": draw_labels(jax.random.fold_in(arg_keys[6], 71), 0),
        "queries": draw_queries(jax.random.fold_in(arg_keys[6], 71), 0),
        "bank": centred(arg_keys[3], (PROTOS, D), D ** -0.5, 0.21875, ((0, 128), (1, 2)), jnp.float32),
        "old_conc": jnp.clip(0.4 + 0.20000002 * jax.random.uniform(arg_keys[4], (PROTOS,), jnp.float32) ** levels(arg_keys[4], (PROTOS,), ((0, 128),), -0.2, 0.2), 0.4, 0.6),
        "neg_index": draw_neg_index(jax.random.fold_in(arg_keys[6], 71), 0),
    }


def reference(features, labels, queries, bank, old_conc, neg_index):
    protos = bank.shape[0]
    feat32 = features.astype(jnp.float32)
    sums = jax.ops.segment_sum(feat32, labels, num_segments=protos)
    counts = jax.ops.segment_sum(jnp.ones(labels.shape, jnp.float32), labels, num_segments=protos)
    touched = counts > 0
    safe_counts = jnp.maximum(counts, 1.0)
    blended = 0.5 * bank + 0.5 * sums / safe_counts[:, None]
    new_bank = jnp.where(touched[:, None], blended, bank)
    differ = feat32 - new_bank[labels]
    dist = jnp.sqrt(lax.optimization_barrier(jnp.sum(differ * differ, axis=1)) + 0.25)
    dist_sums = jax.ops.segment_sum(dist, labels, num_segments=protos)
    new_conc = jnp.where(touched, dist_sums / (safe_counts * jnp.log(safe_counts + 10.0)), old_conc)
    scaled = (new_bank / new_conc[:, None]).astype(jnp.bfloat16)
    negs = scaled[neg_index]
    posrows = scaled[labels]
    positive = lax.optimization_barrier(jnp.sum(queries.astype(jnp.float32) * posrows.astype(jnp.float32), axis=1))
    rows_all = queries.shape[0]
    block = math.gcd(rows_all, 1024)
    blocks = rows_all // block

    def one_block(args):
        query_block, pos_block, prow_block = args
        negative = jnp.dot(query_block, negs.T, preferred_element_type=jnp.float32)
        top = jnp.maximum(lax.optimization_barrier(jnp.max(negative, axis=1)), pos_block)
        expneg = jnp.exp(negative - top[:, None])
        exppos = jnp.exp(pos_block - top)
        total = lax.optimization_barrier(jnp.sum(expneg, axis=1)) + exppos
        loss_block = jnp.log(total) + top - pos_block
        weight = (expneg / total[:, None]).astype(jnp.bfloat16)
        grad_block = jnp.dot(weight, negs, preferred_element_type=jnp.float32)
        grad_block = grad_block + (exppos / total - 1.0)[:, None] * prow_block.astype(jnp.float32)
        return (loss_block, grad_block)
    loss, grad = lax.map(one_block, (queries.reshape(blocks, block, -1), positive.reshape(blocks, block), posrows.reshape(blocks, block, -1)))
    return (new_bank, new_conc, loss.reshape(rows_all), grad.reshape(rows_all, -1))
```

```python
import functools
import jax
import jax.numpy as jnp
from jax import lax
from jax.experimental import pallas as pl
from jax.experimental.pallas import tpu as pltpu
from jax.sharding import PartitionSpec as P

MESH = pl.DeviceIdType.MESH
F32, BF16 = jnp.float32, jnp.bfloat16
LEN = {"x": 4, "y": 4, "z": 8}
CHIPS = 128
OWNED = 1024
ROWS = 256
HALF = 384
CAP = 6
TILE = 256


def iota(shape, dim):
    return lax.broadcasted_iota(jnp.int32, shape, dim)


def peer(me, d):
    return lax.rem(me + d, CHIPS)


def blocks_start(src, dst, to, ssem, rsem, lo, hi, me):
    def go(d, _):
        o = peer(me, d)
        pltpu.make_async_remote_copy(
            src(o), dst(me), ssem, rsem, device_id={"dp": o}, device_id_type=MESH
        ).start()
        return 0

    lax.fori_loop(lo, hi, go, 0)


def wait_send(ref, ssem, rsem):
    pltpu.make_async_remote_copy(
        ref, ref, ssem, rsem, device_id={"dp": 0}, device_id_type=MESH
    ).wait_send()


def wait_recv(ref, ssem, rsem):
    pltpu.make_async_remote_copy(
        ref, ref, ssem, rsem, device_id={"dp": 0}, device_id_type=MESH
    ).wait_recv()


def make_colour(own, gathered, ssem, rsem, at_chip, pending, count):
    def chip(axis, v):
        d = dict(at_chip)
        d[axis] = v
        return (d["y"] * 8 + d["z"]) * 4 + d["x"]

    def off(axis, k):
        return lax.rem(at_chip[axis] + k + LEN[axis], LEN[axis])

    def send(src, dst, to):
        i = count[0]
        count[0] += 1
        copy = pltpu.make_async_remote_copy(
            src, dst, ssem.at[i], rsem.at[i], device_id={"dp": to}, device_id_type=MESH
        )
        copy.start()
        pending.append(copy.wait_send)
        return i

    def arrived(ref, i):
        wait_recv(ref, ssem.at[i], rsem.at[i])

    def colour(order, unit, halves):
        a1, a2, a3 = order
        buffer = gathered[unit]
        layout = "xyz" if unit else "zxy"

        def at(k1, k2, k3, part=None):
            pos = {a1: k1, a2: k2, a3: k3}
            idx = []
            for a in layout:
                n = LEN[a]
                if pos[a] is not None:
                    idx.append(pos[a])
                elif part is None:
                    idx.append(pl.ds(0, n))
                else:
                    idx.append(pl.ds(part * (n // 2), n // 2))
            return buffer.at[tuple(idx) + (halves,)]

        mine = own.at[unit, halves]
        c1, c2, c3 = (at_chip[a] for a in order)
        first = [
            (d, send(mine, at(c1, c2, c3), chip(a1, off(a1, d))))
            for d in range(1, LEN[a1])
        ]
        i = count[0]
        count[0] += 1
        local = pltpu.make_async_copy(mine, at(c1, c2, c3), ssem.at[i])
        local.start()
        yield
        local.wait()
        for d, i in first:
            arrived(at(off(a1, -d), c2, c3), i)
        right2, left2 = chip(a2, off(a2, 1)), chip(a2, off(a2, -1))
        right3, left3 = chip(a3, off(a3, 1)), chip(a3, off(a3, -1))
        last = LEN[a3] // 2
        flying = {}

        def start(k2):
            block = at(None, off(a2, k2), c3)
            flying[k2] = (send(block, block, right3), send(block, block, left3))

        def step(k2, s):
            there = off(a2, k2)
            from_left, from_right = flying[k2]
            part = (0, 1) if s == last else (None, None)
            on = (0, 1) if s + 1 == last else (None, None)
            arrived(at(None, there, off(a3, -s), part[0]), from_left)
            if s < last:
                block = at(None, there, off(a3, -s), on[0])
                i = send(block, block, right3)
            arrived(at(None, there, off(a3, s), part[1]), from_right)
            if s < last:
                block = at(None, there, off(a3, s), on[1])
                flying[k2] = (i, send(block, block, left3))

        block = at(None, c2, c3)
        to_r, to_l = send(block, block, right2), send(block, block, left2)
        start(0)
        yield
        arrived(at(None, off(a2, -1), c3), to_r)
        arrived(at(None, off(a2, 1), c3), to_l)
        block = at(None, off(a2, -1), c3, 0)
        to_r = send(block, block, right2)
        block = at(None, off(a2, 1), c3, 1)
        to_l = send(block, block, left2)
        start(-1)
        start(1)
        yield
        arrived(at(None, off(a2, 2), c3, 0), to_r)
        arrived(at(None, off(a2, 2), c3, 1), to_l)
        start(2)
        yield
        for s in range(1, last + 1):
            for k2 in (0, -1, 1, 2):
                step(k2, s)
            yield

    return colour


def as_column(row, n):
    eye = iota((n, n), 0) == iota((n, n), 1)
    return jnp.sum(jnp.where(eye, row, jnp.zeros_like(row)), axis=1, keepdims=True)


def kernel(
    feat, labels, q, bank, old_conc, negs,
    new_bank, new_conc, loss, grad,
    sent, sent_ids, got, got_ids, back, returned, route, wide,
    d2_mine, d2_theirs, nb16, scaled, count_of, conc_of, mine, own,
    g0, g1, g2, g3, qf, acc, stats, acc_in, stats_in,
    ag_send, ag_recv, sem,
):
    me = lax.axis_index("dp")
    core = lax.axis_index("mp")
    other = 1 - core
    at_chip = {
        "x": lax.rem(me, 4),
        "y": lax.div(me, 32),
        "z": lax.rem(lax.div(me, 4), 8),
    }

    def to_partner(src, dst, k):
        return pltpu.make_async_remote_copy(
            src, dst, sem.at[k], sem.at[k + 1], device_id={"mp": other}, device_id_type=MESH
        )

    def clear(k, _):
        rows = pl.ds(k * 16, 16)
        got[rows, :, 0:HALF] = jnp.zeros((16, 8, HALF), BF16)
        got[rows, :, HALF:] = jnp.ones((16, 8, 128), BF16)
        returned[rows] = jnp.zeros((16, 8, HALF), BF16)
        return 0

    lax.fori_loop(0, CHIPS // 16, clear, 0)

    barrier = pltpu.get_barrier_semaphore()

    def greet(d, _):
        pl.semaphore_signal(
            barrier, inc=1, device_id={"dp": peer(me, d)}, device_id_type=MESH
        )
        return 0

    lax.fori_loop(1, CHIPS, greet, 0)
    pl.semaphore_signal(barrier, inc=1, device_id={"mp": other}, device_id_type=MESH)

    lab_row = labels[...]
    own_row = lax.shift_right_logical(lab_row, 10)
    own_col = as_column(own_row.astype(F32), ROWS).astype(jnp.int32)
    same = own_col == own_row
    r_i, c_i = iota((ROWS, ROWS), 0), iota((ROWS, ROWS), 1)
    rank_row = jnp.sum(jnp.where(same & (r_i < c_i), 1.0, 0.0), axis=0, keepdims=True)
    rank_col = jnp.sum(jnp.where(same & (c_i < r_i), 1.0, 0.0), axis=1, keepdims=True)
    slot_row = own_row * 8 + rank_row.astype(jnp.int32)
    slot_col = own_col * 8 + rank_col.astype(jnp.int32)
    lab_col = as_column(lab_row.astype(F32), ROWS).astype(jnp.int32)
    id_col = jnp.bitwise_and(lab_col, OWNED - 1) + 1
    at_rank = iota((ROWS, 128), 1) == rank_col.astype(jnp.int32)
    hi = jnp.where(at_rank, lax.shift_right_logical(id_col, 5).astype(F32), 0.0).astype(BF16)
    lo = jnp.where(at_rank, jnp.bitwise_and(id_col, 31).astype(F32), 0.0).astype(BF16)
    fv = feat[...]
    for k in range(OWNED // TILE):
        r = iota((TILE, ROWS), 0) + k * TILE
        pick = jnp.where(r == slot_row, 1.0, 0.0).astype(BF16)
        rows = jnp.dot(pick, fv, preferred_element_type=F32).astype(BF16)
        sent[k * 32 : (k + 1) * 32] = rows.reshape(32, 8, HALF)
        pick = jnp.where(r == own_row * 8, 1.0, 0.0).astype(BF16)
        ids = jnp.dot(pick, hi, preferred_element_type=F32) * 32.0
        ids = ids + jnp.dot(pick, lo, preferred_element_type=F32)
        sent_ids[k * 32 : (k + 1) * 32] = ids.reshape(32, 8, 128)
    c = iota((ROWS, OWNED), 1)
    route[...] = jnp.where(c == slot_col, 1.0, 0.0).astype(BF16)

    pl.semaphore_wait(barrier, CHIPS)

    six = pl.ds(0, CAP)
    left = pl.ds(0, HALF)
    blocks_start(
        lambda o: sent_ids.at[o, pl.ds(0, 1)], lambda o: got_ids.at[o, pl.ds(0, 1)],
        None, sem.at[0], sem.at[1], 1, CHIPS, me,
    )
    blocks_start(
        lambda o: sent.at[o, six], lambda o: got.at[o, six, left],
        None, sem.at[2], sem.at[3], 1, CHIPS, me,
    )
    qx = to_partner(q, qf.at[core], 8)
    qx.start()
    home = [
        pltpu.make_async_copy(sent_ids.at[me, pl.ds(0, 1)], got_ids.at[me, pl.ds(0, 1)], sem.at[10]),
        pltpu.make_async_copy(sent.at[me, six], got.at[me, six, left], sem.at[11]),
        pltpu.make_async_copy(q, qf.at[core], sem.at[12]),
    ]
    for copy in home:
        copy.start()
    for copy in home:
        copy.wait()
    rest = pl.ds(0, CHIPS - 1)
    wait_recv(got_ids.at[rest, pl.ds(0, 1)], sem.at[0], sem.at[1])

    spread = jnp.broadcast_to(got_ids[:, 0:1, :], (CHIPS, 8, 128))
    here = iota((CHIPS, 8, 128), 1) == iota((CHIPS, 8, 128), 2)
    id_c = jnp.sum(jnp.where(here, spread, 0.0), axis=2, keepdims=True) - 1.0
    wide[...] = jnp.broadcast_to(id_c, (CHIPS, 8, 128)).reshape(OWNED, 128)
    id_row = jnp.transpose(wide[...])[0:1, :].astype(jnp.int32)
    wait_recv(got.at[rest, six, left], sem.at[2], sem.at[3])

    gv = got[...].reshape(OWNED, HALF + 128)
    for k in range(OWNED // TILE):
        rows = pl.ds(k * TILE, TILE)
        hit = jnp.where(iota((TILE, OWNED), 0) + k * TILE == id_row, 1.0, 0.0).astype(BF16)
        sums = jnp.dot(hit, gv, preferred_element_type=F32)
        counts = sums[:, HALF : HALF + 1]
        old = bank[rows, :]
        mixed = 0.5 * old + 0.5 * sums[:, 0:HALF] / jnp.maximum(counts, 1.0)
        fresh = jnp.where(counts > 0, mixed, old)
        new_bank[rows, :] = fresh
        nb16[rows, :] = fresh.astype(BF16)
        count_of[rows, :] = sums[:, HALF:]

    nbv = nb16[...]
    for k in range(OWNED // TILE):
        rows = pl.ds(k * TILE, TILE)
        ids = wide[rows, :][:, 0:1].astype(jnp.int32)
        hit = jnp.where(iota((TILE, OWNED), 1) == ids, 1.0, 0.0).astype(BF16)
        near = jnp.dot(hit, nbv, preferred_element_type=F32)
        apart = got[k * 32 : (k + 1) * 32, :, 0:HALF].reshape(TILE, HALF).astype(F32) - near
        d2 = jnp.sum(apart * apart, axis=1, keepdims=True)
        d2_mine[:, k * TILE : (k + 1) * TILE] = jnp.transpose(jnp.broadcast_to(d2, (TILE, 128)))[0:8, :]
    d2x = to_partner(d2_mine, d2_theirs, 13)
    d2x.start()
    neg_row = negs[pl.ds(lax.div(me, 2), 1), :]
    want = as_column(neg_row.astype(F32), 128).astype(jnp.int32) - me * OWNED
    old_col = jnp.transpose(jnp.broadcast_to(old_conc[...], (128, OWNED)))
    conc_of[...] = old_col
    d2x.wait()

    dist = jnp.sqrt(d2_mine[0:1, :] + d2_theirs[0:1, :] + 0.25)
    for k in range(OWNED // TILE):
        rows = pl.ds(k * TILE, TILE)
        on = iota((TILE, OWNED), 0) + k * TILE == id_row
        total = jnp.sum(jnp.where(on, dist, 0.0), axis=1, keepdims=True)
        counts = count_of[rows, :][:, 0:1]
        safe = jnp.maximum(counts, 1.0)
        conc = jnp.where(counts > 0, total / (safe * jnp.log(safe + 10.0)), conc_of[rows, :][:, 0:1])
        scaled[rows, :] = (new_bank[rows, :] / conc).astype(BF16)
        conc_of[rows, :] = jnp.broadcast_to(conc, (TILE, 128))

    sv = scaled[...]
    hit = jnp.where(iota((128, OWNED), 1) == want, 1.0, 0.0).astype(BF16)
    mine[...] = jnp.dot(hit, sv, preferred_element_type=F32).astype(BF16).reshape(16, 8, HALF)
    base = lax.rem(me, 2) * 8
    mx = to_partner(mine.at[pl.ds(base + other * 4, 4)], own.at[:, core], 15)
    mx.start()
    keep = pltpu.make_async_copy(mine.at[pl.ds(base + core * 4, 4)], own.at[:, core], sem.at[17])
    keep.start()
    keep.wait()
    new_conc[...] = jnp.transpose(conc_of[...])[0:1, :]
    mx.wait()

    pending = []
    count = [0]
    colour = make_colour(own, (g0, g1, g2, g3), ag_send, ag_recv, at_chip, pending, count)
    both = pl.ds(0, 2)
    live = [
        colour("yxz", 0, both),
        colour("zyx", 1, both),
        colour("zxy", 2, both),
        colour("zyx", 3, pl.ds(0, 1)),
        colour("zxy", 3, pl.ds(1, 1)),
    ]

    def advance():
        for g in list(live):
            try:
                next(g)
            except StopIteration:
                live.remove(g)

    advance()

    for k in range(OWNED // TILE):
        rows = pl.ds(k * TILE, TILE)
        ids = wide[rows, :][:, 0:1].astype(jnp.int32)
        hit = jnp.where(iota((TILE, OWNED), 1) == ids, 1.0, 0.0).astype(BF16)
        out = jnp.dot(hit, sv, preferred_element_type=F32).astype(BF16)
        back[k * 32 : (k + 1) * 32] = out.reshape(32, 8, HALF)
    advance()
    blocks_start(
        lambda o: back.at[o, six], lambda o: returned.at[o, six],
        None, sem.at[4], sem.at[5], 1, CHIPS, me,
    )
    copy = pltpu.make_async_copy(back.at[me, six], returned.at[me, six], sem.at[18])
    copy.start()
    copy.wait()
    qx.wait()
    stats[...] = jnp.full((ROWS, 128), -3.0e38, F32)
    acc[...] = jnp.zeros((2, ROWS, HALF), F32)
    while live:
        advance()

    q0, q1 = qf[0], qf[1]
    top = jnp.full((ROWS, 1), -3.0e38, F32)
    sums = jnp.zeros((ROWS, 1), F32)
    nt = (((1,), (1,)), ((), ()))
    for g in (g0, g1, g2, g3):
        if g is g0:
            plan = [(pl.ds(2 * k, 2),) for k in range(4)]
        else:
            plan = [(pl.ds(k, 1),) for k in range(4)]

        for (part,) in plan:
            k0 = g[part, :, :, 0].reshape(TILE, HALF)
            k1 = g[part, :, :, 1].reshape(TILE, HALF)
            s = lax.dot_general(q0, k0, nt, preferred_element_type=F32)
            s = s + lax.dot_general(q1, k1, nt, preferred_element_type=F32)
            higher = jnp.maximum(top, jnp.max(s, axis=1, keepdims=True))
            shrink = jnp.exp(top - higher)
            p = jnp.exp(s - higher)
            sums = sums * shrink + jnp.sum(p, axis=1, keepdims=True)
            pb = p.astype(BF16)
            acc[0] = acc[0] * shrink + jnp.dot(pb, k0, preferred_element_type=F32)
            acc[1] = acc[1] * shrink + jnp.dot(pb, k1, preferred_element_type=F32)
            top = higher

    wait_recv(returned.at[rest, six], sem.at[4], sem.at[5])
    pos_rows = jnp.dot(
        route[...], returned[...].reshape(OWNED, HALF), preferred_element_type=F32
    )
    part = jnp.sum(q[...].astype(F32) * pos_rows, axis=1, keepdims=True)
    lane = iota((ROWS, 128), 1)
    stats[...] = jnp.where(lane == 0, top, jnp.where(lane == 1, sums, part))
    ax = to_partner(acc.at[other], acc_in, 19)
    sx = to_partner(stats, stats_in, 21)
    ax.start()
    sx.start()
    ax.wait()
    sx.wait()
    t2, s2, p2 = stats_in[:, 0:1], stats_in[:, 1:2], stats_in[:, 2:3]
    positive = part + p2
    peak = jnp.maximum(jnp.maximum(top, t2), positive)
    w1, w2, wp = jnp.exp(top - peak), jnp.exp(t2 - peak), jnp.exp(positive - peak)
    total = sums * w1 + s2 * w2 + wp
    lcol = jnp.log(total) + peak - positive
    loss[...] = jnp.transpose(jnp.broadcast_to(lcol, (ROWS, 128)))[0:1, :]
    grad[...] = (
        (acc[core] * w1 + acc_in[...] * w2) / total + (wp / total - 1.0) * pos_rows
    )

    for wait in pending:
        wait()
    wait_send(sent_ids.at[rest, pl.ds(0, 1)], sem.at[0], sem.at[1])
    wait_send(sent.at[rest, six], sem.at[2], sem.at[3])
    wait_send(back.at[rest, six], sem.at[4], sem.at[5])


def body(features, labels, queries, bank, old_conc, neg_index):
    vmem = pl.BlockSpec(memory_space=pltpu.VMEM)
    big = (4, 4, 8, 2, 8, HALF)
    outs = pl.pallas_call(
        kernel,
        out_shape=(
            jax.ShapeDtypeStruct((OWNED, HALF), F32),
            jax.ShapeDtypeStruct((1, OWNED), F32),
            jax.ShapeDtypeStruct((1, ROWS), F32),
            jax.ShapeDtypeStruct((ROWS, HALF), F32),
        ),
        in_specs=[vmem] * 6,
        out_specs=(vmem,) * 4,
        scratch_shapes=[
            pltpu.VMEM((CHIPS, 8, HALF), BF16),
            pltpu.VMEM((CHIPS, 8, 128), F32),
            pltpu.VMEM((CHIPS, 8, HALF + 128), BF16),
            pltpu.VMEM((CHIPS, 8, 128), F32),
            pltpu.VMEM((CHIPS, 8, HALF), BF16),
            pltpu.VMEM((CHIPS, 8, HALF), BF16),
            pltpu.VMEM((ROWS, OWNED), BF16),
            pltpu.VMEM((OWNED, 128), F32),
            pltpu.VMEM((8, OWNED), F32),
            pltpu.VMEM((8, OWNED), F32),
            pltpu.VMEM((OWNED, HALF), BF16),
            pltpu.VMEM((OWNED, HALF), BF16),
            pltpu.VMEM((OWNED, 128), F32),
            pltpu.VMEM((OWNED, 128), F32),
            pltpu.VMEM((16, 8, HALF), BF16),
            pltpu.VMEM((4, 2, 8, HALF), BF16),
            pltpu.VMEM((8, 4, 4, 2, 8, HALF), BF16),
            pltpu.VMEM(big, BF16),
            pltpu.VMEM(big, BF16),
            pltpu.VMEM(big, BF16),
            pltpu.VMEM((2, ROWS, HALF), BF16),
            pltpu.VMEM((2, ROWS, HALF), F32),
            pltpu.VMEM((ROWS, 128), F32),
            pltpu.VMEM((ROWS, HALF), F32),
            pltpu.VMEM((ROWS, 128), F32),
            pltpu.SemaphoreType.DMA((160,)),
            pltpu.SemaphoreType.DMA((160,)),
            pltpu.SemaphoreType.DMA((24,)),
        ],
        compiler_params=pltpu.CompilerParams(
            collective_id=0, has_side_effects=True, vmem_limit_bytes=60 << 20
        ),
        name="step",
    )(
        features,
        labels.reshape(1, ROWS),
        queries,
        bank,
        old_conc.reshape(1, OWNED),
        neg_index.reshape(64, 128),
    )
    new_bank, new_conc, loss, grad = outs
    return new_bank, new_conc.reshape(OWNED), loss.reshape(ROWS), grad


def solution(mesh):
    return jax.shard_map(
        body,
        mesh=mesh,
        in_specs=(P("dp", "mp"), P("dp"), P("dp", "mp"), P("dp", "mp"), P("dp"), P()),
        out_specs=(P("dp", "mp"), P("dp"), P("dp"), P("dp", "mp")),
        check_vma=False,
    )
```

```python
import functools
import jax
import jax.numpy as jnp
from jax import lax
from jax.experimental import pallas as pl
from jax.experimental.pallas import tpu as pltpu
from jax.sharding import PartitionSpec as P

MESH = pl.DeviceIdType.MESH
F32, BF16 = jnp.float32, jnp.bfloat16
LEN = {"x": 4, "y": 4, "z": 8}
CHIPS = 128
OWNED = 1024
ROWS = 256
HALF = 384
CAP = 6
SHARE = 128
TILE = 256


def iota(shape, dim):
    return lax.broadcasted_iota(jnp.int32, shape, dim)


def peer(me, d):
    return lax.rem(me + d, CHIPS)


def blocks_start(src, dst, ssem, rsem, me):
    def go(d, _):
        o = peer(me, d)
        pltpu.make_async_remote_copy(
            src(o), dst(me), ssem, rsem, device_id={"dp": o}, device_id_type=MESH
        ).start()
        return 0

    lax.fori_loop(1, CHIPS, go, 0)


def wait_send(ref, ssem, rsem):
    pltpu.make_async_remote_copy(
        ref, ref, ssem, rsem, device_id={"dp": 0}, device_id_type=MESH
    ).wait_send()


def wait_recv(ref, ssem, rsem):
    pltpu.make_async_remote_copy(
        ref, ref, ssem, rsem, device_id={"dp": 0}, device_id_type=MESH
    ).wait_recv()


def make_colour(own, shards, core, ssem, rsem, at_chip, pending, count):
    def chip(axis, v):
        d = dict(at_chip)
        d[axis] = v
        return (d["y"] * 8 + d["z"]) * 4 + d["x"]

    def off(axis, k):
        return lax.rem(at_chip[axis] + k + LEN[axis], LEN[axis])

    def send(src, dst, **to):
        i = count[0]
        count[0] += 1
        copy = pltpu.make_async_remote_copy(
            src, dst, ssem.at[i], rsem.at[i], device_id=to, device_id_type=MESH
        )
        copy.start()
        pending.append(copy.wait_send)
        return i

    def arrived(ref, i):
        wait_recv(ref, ssem.at[i], rsem.at[i])

    def colour(first, second, unit):
        gathered, theirs = shards[unit].at[core], shards[unit].at[1 - core]
        c1, c2 = at_chip[first], at_chip[second]
        last = LEN[second] // 2
        n = LEN[first]

        def at(k, part=None, ref=None):
            ref = gathered if ref is None else ref
            if part is None:
                return ref.at[off(second, k)]
            return ref.at[off(second, k), pl.ds(part * (n // 2), n // 2)]

        def hand_over(k, part=None):
            block = at(k, part)
            handed.append((at(k, part, theirs), send(block, block, mp=1 - core)))

        handed = []
        mine = own[unit]
        away = [
            (d, send(mine, gathered.at[c2, c1], dp=chip(first, off(first, d))))
            for d in range(1, n)
        ]
        i = count[0]
        count[0] += 1
        local = pltpu.make_async_copy(mine, gathered.at[c2, c1], ssem.at[i])
        local.start()
        yield
        local.wait()
        for d, i in away:
            arrived(gathered.at[c2, off(first, -d)], i)
        right, left = chip(second, off(second, 1)), chip(second, off(second, -1))
        from_left, from_right = send(at(0), at(0), dp=right), send(at(0), at(0), dp=left)
        hand_over(0)
        yield
        for s in range(1, last + 1):
            part = (0, 1) if s == last else (None, None)
            on = (0, 1) if s + 1 == last else (None, None)
            arrived(at(-s, part[0]), from_left)
            if s < last:
                from_left = send(at(-s, on[0]), at(-s, on[0]), dp=right)
            arrived(at(s, part[1]), from_right)
            if s < last:
                from_right = send(at(s, on[1]), at(s, on[1]), dp=left)
            hand_over(-s, part[0])
            hand_over(s, part[1])
            yield
        for ref, i in handed:
            arrived(ref, i)

    return colour


def as_column(row, n):
    eye = iota((n, n), 0) == iota((n, n), 1)
    return jnp.sum(jnp.where(eye, row, jnp.zeros_like(row)), axis=1, keepdims=True)


def kernel(
    feat, labels, q, bank_in, old_conc, negs,
    bank_out, new_conc, loss, grad,
    bank, new_bank,
    sent, sent_ids, got, got_ids, back, returned, route, wide,
    d2_mine, d2_theirs, nb16, scaled, count_of, conc_of, mine, own0, own1,
    g0, g1, qf, acc, acc16, acc_in, stats, stats_in, pos_mine, pos_theirs,
    ag_send, ag_recv, sem,
):
    me = lax.axis_index("dp")
    core = lax.axis_index("mp")
    other = 1 - core
    at_chip = {
        "x": lax.rem(me, 4),
        "y": lax.div(me, 32),
        "z": lax.rem(lax.div(me, 4), 8),
    }

    def to_partner(src, dst, k):
        return pltpu.make_async_remote_copy(
            src, dst, sem.at[k], sem.at[k + 1], device_id={"mp": other}, device_id_type=MESH
        )

    barrier = pltpu.get_barrier_semaphore()

    def greet(d, _):
        pl.semaphore_signal(
            barrier, inc=1, device_id={"dp": peer(me, d)}, device_id_type=MESH
        )
        return 0

    lax.fori_loop(1, CHIPS, greet, 0)
    pl.semaphore_signal(barrier, inc=1, device_id={"mp": other}, device_id_type=MESH)
    beside = [
        at_chip["y"] * 32 + at_chip["z"] * 4 + lax.rem(at_chip["x"] + d, 4) for d in (1, 2, 3)
    ]
    for chip in beside:
        pl.semaphore_signal(
            barrier, inc=1, device_id={"dp": chip, "mp": other}, device_id_type=MESH
        )

    read_bank = pltpu.make_async_copy(bank_in, bank, sem.at[19])
    read_bank.start()

    def clear(k, _):
        rows = pl.ds(k * 16, 16)
        got[rows, CAP:8, 0:HALF] = jnp.zeros((16, 2, HALF), BF16)
        got[rows, :, HALF:] = jnp.ones((16, 8, 128), BF16)
        returned[rows, CAP:8, :] = jnp.zeros((16, 2, HALF), BF16)
        return 0

    lax.fori_loop(0, CHIPS // 16, clear, 0)

    lab_row = labels[...]
    own_row = lax.shift_right_logical(lab_row, 10)
    own_col = as_column(own_row.astype(F32), ROWS).astype(jnp.int32)
    same = own_col == own_row
    r_i, c_i = iota((ROWS, ROWS), 0), iota((ROWS, ROWS), 1)
    rank_row = jnp.sum(jnp.where(same & (r_i < c_i), 1.0, 0.0), axis=0, keepdims=True)
    rank_col = jnp.sum(jnp.where(same & (c_i < r_i), 1.0, 0.0), axis=1, keepdims=True)
    slot_row = own_row * 8 + rank_row.astype(jnp.int32)
    slot_col = own_col * 8 + rank_col.astype(jnp.int32)
    lab_col = as_column(lab_row.astype(F32), ROWS).astype(jnp.int32)
    id_col = jnp.bitwise_and(lab_col, OWNED - 1) + 1
    at_rank = iota((ROWS, 128), 1) == rank_col.astype(jnp.int32)
    hi = jnp.where(at_rank, lax.shift_right_logical(id_col, 5).astype(F32), 0.0).astype(BF16)
    lo = jnp.where(at_rank, jnp.bitwise_and(id_col, 31).astype(F32), 0.0).astype(BF16)
    fv = feat[...]
    for k in range(OWNED // TILE):
        r = iota((TILE, ROWS), 0) + k * TILE
        pick = jnp.where(r == slot_row, 1.0, 0.0).astype(BF16)
        rows = jnp.dot(pick, fv, preferred_element_type=F32).astype(BF16)
        sent[k * 32 : (k + 1) * 32] = rows.reshape(32, 8, HALF)
        pick = jnp.where(r == own_row * 8, 1.0, 0.0).astype(BF16)
        ids = jnp.dot(pick, hi, preferred_element_type=F32) * 32.0
        ids = ids + jnp.dot(pick, lo, preferred_element_type=F32)
        sent_ids[k * 32 : (k + 1) * 32] = ids.reshape(32, 8, 128)
    c = iota((ROWS, OWNED), 1)
    route[...] = jnp.where(c == slot_col, 1.0, 0.0).astype(BF16)

    pl.semaphore_wait(barrier, CHIPS + 3)

    six = pl.ds(0, CAP)
    left = pl.ds(0, HALF)
    blocks_start(
        lambda o: sent_ids.at[o, pl.ds(0, 1)], lambda o: got_ids.at[o, pl.ds(0, 1)],
        sem.at[0], sem.at[1], me,
    )
    blocks_start(
        lambda o: sent.at[o, six], lambda o: got.at[o, six, left],
        sem.at[2], sem.at[3], me,
    )
    x = at_chip["x"]
    for chip in beside:
        for c in range(2):
            pltpu.make_async_remote_copy(
                q.at[c], qf.at[core * 4 + x], sem.at[8], sem.at[9],
                device_id={"dp": chip, "mp": c}, device_id_type=MESH,
            ).start()
    to_partner(q.at[other], qf.at[core * 4 + x], 8).start()
    home = [
        pltpu.make_async_copy(sent_ids.at[me, pl.ds(0, 1)], got_ids.at[me, pl.ds(0, 1)], sem.at[10]),
        pltpu.make_async_copy(sent.at[me, six], got.at[me, six, left], sem.at[11]),
        pltpu.make_async_copy(q.at[core], qf.at[core * 4 + x], sem.at[12]),
    ]
    for copy in home:
        copy.start()
    for copy in home:
        copy.wait()
    rest = pl.ds(0, CHIPS - 1)
    wait_recv(got_ids.at[rest, pl.ds(0, 1)], sem.at[0], sem.at[1])

    spread = jnp.broadcast_to(got_ids[:, 0:1, :], (CHIPS, 8, 128))
    here = iota((CHIPS, 8, 128), 1) == iota((CHIPS, 8, 128), 2)
    id_c = jnp.sum(jnp.where(here, spread, 0.0), axis=2, keepdims=True) - 1.0
    wide[...] = jnp.broadcast_to(id_c, (CHIPS, 8, 128)).reshape(OWNED, 128)
    id_row = jnp.transpose(wide[...])[0:1, :].astype(jnp.int32)
    wait_recv(got.at[rest, six, left], sem.at[2], sem.at[3])

    read_bank.wait()
    gv = got[...].reshape(OWNED, HALF + 128)
    for k in range(OWNED // TILE):
        rows = pl.ds(k * TILE, TILE)
        hit = jnp.where(iota((TILE, OWNED), 0) + k * TILE == id_row, 1.0, 0.0).astype(BF16)
        sums = jnp.dot(hit, gv, preferred_element_type=F32)
        counts = sums[:, HALF : HALF + 1]
        old = bank[rows, :]
        mixed = 0.5 * old + 0.5 * sums[:, 0:HALF] / jnp.maximum(counts, 1.0)
        fresh = jnp.where(counts > 0, mixed, old)
        new_bank[rows, :] = fresh
        nb16[rows, :] = fresh.astype(BF16)
        count_of[rows, :] = sums[:, HALF:]

    nbv = nb16[...]
    for k in range(OWNED // TILE):
        rows = pl.ds(k * TILE, TILE)
        ids = wide[rows, :][:, 0:1].astype(jnp.int32)
        hit = jnp.where(iota((TILE, OWNED), 1) == ids, 1.0, 0.0).astype(BF16)
        near = jnp.dot(hit, nbv, preferred_element_type=F32)
        apart = got[k * 32 : (k + 1) * 32, :, 0:HALF].reshape(TILE, HALF).astype(F32) - near
        d2 = jnp.sum(apart * apart, axis=1, keepdims=True)
        d2_mine[:, k * TILE : (k + 1) * TILE] = jnp.transpose(jnp.broadcast_to(d2, (TILE, 128)))[0:8, :]
    write_bank = pltpu.make_async_copy(new_bank, bank_out, sem.at[20])
    write_bank.start()
    d2x = to_partner(d2_mine, d2_theirs, 13)
    d2x.start()
    neg_row = negs[pl.ds(lax.div(me, 2), 1), :]
    want = as_column(neg_row.astype(F32), 128).astype(jnp.int32) - me * OWNED
    old_col = jnp.transpose(jnp.broadcast_to(old_conc[...], (128, OWNED)))
    conc_of[...] = old_col
    d2x.wait()

    dist = jnp.sqrt(d2_mine[0:1, :] + d2_theirs[0:1, :] + 0.25)
    for k in range(OWNED // TILE):
        rows = pl.ds(k * TILE, TILE)
        on = iota((TILE, OWNED), 0) + k * TILE == id_row
        total = jnp.sum(jnp.where(on, dist, 0.0), axis=1, keepdims=True)
        counts = count_of[rows, :][:, 0:1]
        safe = jnp.maximum(counts, 1.0)
        conc = jnp.where(counts > 0, total / (safe * jnp.log(safe + 10.0)), conc_of[rows, :][:, 0:1])
        scaled[rows, :] = (new_bank[rows, :] / conc).astype(BF16)
        conc_of[rows, :] = jnp.broadcast_to(conc, (TILE, 128))

    sv = scaled[...]
    hit = jnp.where(iota((128, OWNED), 1) == want, 1.0, 0.0).astype(BF16)
    mine[...] = jnp.dot(hit, sv, preferred_element_type=F32).astype(BF16).reshape(8, 16, HALF)
    base = lax.rem(me, 2) * 4
    swap = []
    for k, own in enumerate((own0, own1)):
        swap.append(to_partner(mine.at[base + other * 2 + k], own.at[core], 21 + 2 * k))
        swap[-1].start()
    keep = [
        pltpu.make_async_copy(mine.at[base + core * 2 + k], own.at[core], sem.at[15 + k])
        for k, own in enumerate((own0, own1))
    ]
    for copy in keep:
        copy.start()
    for copy in keep:
        copy.wait()
    new_conc[...] = jnp.transpose(conc_of[...])[0:1, :]
    for copy in swap:
        copy.wait()

    pending = []
    count = [0]
    colour = make_colour((own0, own1), (g0, g1), core, ag_send, ag_recv, at_chip, pending, count)
    live = [colour("z", "y", 0), colour("y", "z", 1)]

    def advance():
        for g in list(live):
            try:
                next(g)
            except StopIteration:
                live.remove(g)

    advance()

    for k in range(OWNED // TILE):
        rows = pl.ds(k * TILE, TILE)
        ids = wide[rows, :][:, 0:1].astype(jnp.int32)
        hit = jnp.where(iota((TILE, OWNED), 1) == ids, 1.0, 0.0).astype(BF16)
        out = jnp.dot(hit, sv, preferred_element_type=F32).astype(BF16)
        back[k * 32 : (k + 1) * 32] = out.reshape(32, 8, HALF)
    advance()
    blocks_start(
        lambda o: back.at[o, six], lambda o: returned.at[o, six],
        sem.at[4], sem.at[5], me,
    )
    copy = pltpu.make_async_copy(back.at[me, six], returned.at[me, six], sem.at[18])
    copy.start()
    copy.wait()
    while live:
        advance()

    seven = qf.at[pl.ds(0, 7)]
    wait_recv(seven, sem.at[8], sem.at[9])
    wait_send(seven, sem.at[8], sem.at[9])
    many = 4 * SHARE
    q0, q1 = qf[0:4].reshape(many, HALF), qf[4:8].reshape(many, HALF)
    top = jnp.full((many, 1), -3.0e38, F32)
    sums = jnp.zeros((many, 1), F32)
    acc[...] = jnp.zeros((2, many, HALF), F32)
    nt = (((1,), (1,)), ((), ()))
    for g, planes, width in ((g0, 4, 1), (g1, 4, 2)):
        for k in range(planes):
            part = pl.ds(k * width, width)
            k0 = g[:, part, :, 0].reshape(TILE, HALF)
            k1 = g[:, part, :, 1].reshape(TILE, HALF)
            s = lax.dot_general(q0, k0, nt, preferred_element_type=F32)
            s = s + lax.dot_general(q1, k1, nt, preferred_element_type=F32)
            higher = jnp.maximum(top, jnp.max(s, axis=1, keepdims=True))
            shrink = jnp.exp(top - higher)
            p = jnp.exp(s - higher)
            sums = sums * shrink + jnp.sum(p, axis=1, keepdims=True)
            pb = p.astype(BF16)
            acc[0] = acc[0] * shrink + jnp.dot(pb, k0, preferred_element_type=F32)
            acc[1] = acc[1] * shrink + jnp.dot(pb, k1, preferred_element_type=F32)
            top = higher
    acc16[...] = acc[...].astype(BF16).reshape(2, 4, SHARE, HALF)
    lane = iota((many, 128), 1)
    both = jnp.transpose(jnp.where(lane == 0, top, sums))
    for k in range(4):
        stats[k] = both[0:8, k * SHARE : (k + 1) * SHARE]

    for chip, d in zip(beside, (1, 2, 3)):
        there = lax.rem(x + d, 4)
        for h in range(2):
            to = {"dp": chip, "mp": h}
            pltpu.make_async_remote_copy(
                stats.at[there], stats_in.at[x * 2 + core], sem.at[27], sem.at[28], device_id=to, device_id_type=MESH
            ).start()
            pltpu.make_async_remote_copy(
                acc16.at[h, there], acc_in.at[x * 2 + core], sem.at[25], sem.at[26], device_id=to, device_id_type=MESH
            ).start()
    to_partner(stats.at[x], stats_in.at[x * 2 + core], 27).start()
    to_partner(acc16.at[other, x], acc_in.at[x * 2 + core], 25).start()
    keep = [
        pltpu.make_async_copy(stats.at[x], stats_in.at[x * 2 + core], sem.at[29]),
        pltpu.make_async_copy(acc16.at[core, x], acc_in.at[x * 2 + core], sem.at[30]),
    ]
    for copy in keep:
        copy.start()

    wait_recv(returned.at[rest, six], sem.at[4], sem.at[5])
    pos_rows = jnp.dot(
        route[...], returned[...].reshape(OWNED, HALF), preferred_element_type=F32
    )
    part = jnp.sum(q[...].reshape(ROWS, HALF).astype(F32) * pos_rows, axis=1, keepdims=True)
    pos_mine[...] = jnp.transpose(jnp.broadcast_to(part, (ROWS, 128)))[0:8, :]
    px = to_partner(pos_mine, pos_theirs, 31)
    px.start()
    px.wait()
    positive_row = pos_mine[0:1, :] + pos_theirs[0:1, :]
    for copy in keep:
        copy.wait()
    for ref, k in ((stats_in, 27), (acc_in, 25)):
        wait_recv(ref.at[pl.ds(0, 7)], sem.at[k], sem.at[k + 1])
        wait_send(ref.at[pl.ds(0, 7)], sem.at[k], sem.at[k + 1])
    for c in range(2):
        rows = slice(c * SHARE, (c + 1) * SHARE)
        positive = positive_row[:, rows]
        tops = [stats_in[k * 2 + c, 0:1, :] for k in range(4)]
        peak = positive
        for t in tops:
            peak = jnp.maximum(peak, t)
        weights = [jnp.exp(t - peak) for t in tops]
        wp = jnp.exp(positive - peak)
        total = wp
        for k in range(4):
            total = total + stats_in[k * 2 + c, 1:2, :] * weights[k]
        loss[:, rows] = jnp.log(total) + peak - positive
        out = as_column(wp / total - 1.0, SHARE) * pos_rows[rows]
        for k in range(4):
            out = out + as_column(weights[k] / total, SHARE) * acc_in[k * 2 + c].astype(F32)
        grad[rows, :] = out

    write_bank.wait()
    for wait in pending:
        wait()
    wait_send(sent_ids.at[rest, pl.ds(0, 1)], sem.at[0], sem.at[1])
    wait_send(sent.at[rest, six], sem.at[2], sem.at[3])
    wait_send(back.at[rest, six], sem.at[4], sem.at[5])


def body(features, labels, queries, bank, old_conc, neg_index):
    vmem = pl.BlockSpec(memory_space=pltpu.VMEM)
    hbm = pl.BlockSpec(memory_space=pl.ANY)
    outs = pl.pallas_call(
        kernel,
        out_shape=(
            jax.ShapeDtypeStruct((OWNED, HALF), F32),
            jax.ShapeDtypeStruct((1, OWNED), F32),
            jax.ShapeDtypeStruct((1, ROWS), F32),
            jax.ShapeDtypeStruct((ROWS, HALF), F32),
        ),
        in_specs=[vmem, vmem, vmem, hbm, vmem, vmem],
        out_specs=(hbm, vmem, vmem, vmem),
        scratch_shapes=[
            pltpu.VMEM((OWNED, HALF), F32),
            pltpu.VMEM((OWNED, HALF), F32),
            pltpu.VMEM((CHIPS, 8, HALF), BF16),
            pltpu.VMEM((CHIPS, 8, 128), F32),
            pltpu.VMEM((CHIPS, 8, HALF + 128), BF16),
            pltpu.VMEM((CHIPS, 8, 128), F32),
            pltpu.VMEM((CHIPS, 8, HALF), BF16),
            pltpu.VMEM((CHIPS, 8, HALF), BF16),
            pltpu.VMEM((ROWS, OWNED), BF16),
            pltpu.VMEM((OWNED, 128), F32),
            pltpu.VMEM((8, OWNED), F32),
            pltpu.VMEM((8, OWNED), F32),
            pltpu.VMEM((OWNED, HALF), BF16),
            pltpu.VMEM((OWNED, HALF), BF16),
            pltpu.VMEM((OWNED, 128), F32),
            pltpu.VMEM((OWNED, 128), F32),
            pltpu.VMEM((8, 16, HALF), BF16),
            pltpu.VMEM((2, 16, HALF), BF16),
            pltpu.VMEM((2, 16, HALF), BF16),
            pltpu.VMEM((2, 4, 8, 2, 16, HALF), BF16),
            pltpu.VMEM((2, 8, 4, 2, 16, HALF), BF16),
            pltpu.VMEM((8, SHARE, HALF), BF16),
            pltpu.VMEM((2, 4 * SHARE, HALF), F32),
            pltpu.VMEM((2, 4, SHARE, HALF), BF16),
            pltpu.VMEM((8, SHARE, HALF), BF16),
            pltpu.VMEM((4, 8, SHARE), F32),
            pltpu.VMEM((8, 8, SHARE), F32),
            pltpu.VMEM((8, ROWS), F32),
            pltpu.VMEM((8, ROWS), F32),
            pltpu.SemaphoreType.DMA((64,)),
            pltpu.SemaphoreType.DMA((64,)),
            pltpu.SemaphoreType.DMA((40,)),
        ],
        compiler_params=pltpu.CompilerParams(
            collective_id=0, has_side_effects=True, vmem_limit_bytes=32 << 20
        ),
        name="step",
    )(
        features,
        labels.reshape(1, ROWS),
        queries.reshape(2, SHARE, HALF),
        bank,
        old_conc.reshape(1, OWNED),
        neg_index.reshape(64, 128),
    )
    new_bank, new_conc, loss, grad = outs
    return new_bank, new_conc.reshape(OWNED), loss.reshape(ROWS), grad


def solution(mesh):
    return jax.shard_map(
        body,
        mesh=mesh,
        in_specs=(P("dp", "mp"), P("dp"), P("dp", "mp"), P("dp", "mp"), P("dp"), P()),
        out_specs=(P("dp", "mp"), P("dp"), P("dp"), P("dp", "mp")),
        check_vma=False,
    )
```

```python
import functools
import jax
import jax.numpy as jnp
from jax import lax
from jax.experimental import pallas as pl
from jax.experimental.pallas import tpu as pltpu
from jax.sharding import PartitionSpec as P

MESH = pl.DeviceIdType.MESH
F32, BF16 = jnp.float32, jnp.bfloat16
LEN = {"x": 4, "y": 4, "z": 8}
CHIPS = 128
OWNED = 1024
ROWS = 256
HALF = 384
CAP = 6
SHARE = 128
TILE = 256


def iota(shape, dim):
    return lax.broadcasted_iota(jnp.int32, shape, dim)


def peer(me, d):
    return lax.rem(me + d, CHIPS)


def blocks_start(src, dst, ssem, rsem, me):
    def go(d, _):
        o = peer(me, d)
        pltpu.make_async_remote_copy(
            src(o), dst(me), ssem, rsem, device_id={"dp": o}, device_id_type=MESH
        ).start()
        return 0

    lax.fori_loop(1, CHIPS, go, 0)


def wait_send(ref, ssem, rsem):
    pltpu.make_async_remote_copy(
        ref, ref, ssem, rsem, device_id={"dp": 0}, device_id_type=MESH
    ).wait_send()


def wait_recv(ref, ssem, rsem):
    pltpu.make_async_remote_copy(
        ref, ref, ssem, rsem, device_id={"dp": 0}, device_id_type=MESH
    ).wait_recv()


def gather_rounds(mine, gathered, theirs, core, ssem, rsem, at_chip, pending):
    count = [0]
    lengths = {"y": LEN["y"], "z": LEN["z"]}

    def off(axis, k):
        return lax.rem(at_chip[axis] + k + lengths[axis], lengths[axis])

    def chip(axis, k):
        d = dict(at_chip)
        d[axis] = off(axis, k)
        return (d["y"] * 8 + d["z"]) * 4 + d["x"]

    def send(src, dst, **to):
        i = count[0]
        count[0] += 1
        copy = pltpu.make_async_remote_copy(
            src, dst, ssem.at[i], rsem.at[i], device_id=to, device_id_type=MESH
        )
        copy.start()
        pending.append(copy.wait_send)
        return i

    def arrived(ref, i):
        wait_recv(ref, ssem.at[i], rsem.at[i])

    def at(y, z, half=None, ref=gathered):
        ref = ref.at[off("y", y), off("z", z)]
        return ref if half is None else ref.at[half]

    handed = []

    def hand_over(y, z):
        handed.append((at(y, z, ref=theirs), send(at(y, z), at(y, z), mp=1 - core)))

    flying = {}

    def along_y(z, src=None):
        src = at(0, z) if src is None else src
        flying[z] = (send(src, at(0, z), dp=chip("y", 1)), send(src, at(0, z), dp=chip("y", -1)))

    def on_y(z):
        arrived(at(-1, z), flying[z][0])
        right = send(at(-1, z, 0), at(-1, z, 0), dp=chip("y", 1))
        arrived(at(1, z), flying[z][1])
        flying[z] = (right, send(at(1, z, 1), at(1, z, 1), dp=chip("y", -1)))
        hand_over(-1, z)
        hand_over(1, z)

    def end_y(z):
        arrived(at(2, z, 0), flying[z][0])
        arrived(at(2, z, 1), flying[z][1])
        hand_over(2, z)

    up, down = chip("z", 1), chip("z", -1)
    from_down, from_up = send(mine, at(0, 0), dp=up), send(mine, at(0, 0), dp=down)
    along_y(0, mine)
    i = count[0]
    count[0] += 1
    local = pltpu.make_async_copy(mine, at(0, 0), ssem.at[i])
    local.start()
    local.wait()
    hand_over(0, 0)
    yield
    for s in (1, 2, 3):
        part = (0, 1) if s == 3 else (None, None)
        arrived(at(0, -s), from_down)
        from_down = send(at(0, -s, part[0]), at(0, -s, part[0]), dp=up)
        arrived(at(0, s), from_up)
        from_up = send(at(0, s, part[1]), at(0, s, part[1]), dp=down)
        along_y(-s)
        along_y(s)
        hand_over(0, -s)
        hand_over(0, s)
        for z in ((0,), (-1, 1), (-2, 2))[s - 1]:
            on_y(z)
        yield
    arrived(at(0, 4, 0), from_down)
    arrived(at(0, 4, 1), from_up)
    along_y(4)
    hand_over(0, 4)
    for z in (-3, 3):
        on_y(z)
    for z in (0, -1, 1):
        end_y(z)
    on_y(4)
    yield
    for z in (-2, 2, -3, 3, 4):
        end_y(z)
    for ref, i in handed:
        arrived(ref, i)


def as_column(row, n):
    eye = iota((n, n), 0) == iota((n, n), 1)
    return jnp.sum(jnp.where(eye, row, jnp.zeros_like(row)), axis=1, keepdims=True)


def kernel(
    feat_in, labels_in, q_in, bank_in, old_conc_in, negs_in,
    new_bank, new_conc, loss, grad,
    feat, labels, q, bank, old_conc, negs,
    sent, sent_ids, got, got_ids, back, returned, route, wide,
    d2_mine, d2_theirs, nb16, scaled, count_of, conc_of, mine, own,
    shards, qf, acc, acc16, acc_in, stats, stats_in, pos_mine, pos_theirs,
    ag_send, ag_recv, sem,
):
    me = lax.axis_index("dp")
    core = lax.axis_index("mp")
    other = 1 - core
    at_chip = {
        "x": lax.rem(me, 4),
        "y": lax.div(me, 32),
        "z": lax.rem(lax.div(me, 4), 8),
    }

    def to_partner(src, dst, k):
        return pltpu.make_async_remote_copy(
            src, dst, sem.at[k], sem.at[k + 1], device_id={"mp": other}, device_id_type=MESH
        )

    reads = [
        pltpu.make_async_copy(src, dst, sem.at[k])
        for src, dst, k in (
            (labels_in, labels, 33), (feat_in, feat, 34), (q_in, q, 35),
            (old_conc_in, old_conc, 36), (negs_in, negs, 37), (bank_in, bank, 38),
        )
    ]
    for copy in reads:
        copy.start()

    barrier = pltpu.get_barrier_semaphore()

    hops = sorted(
        ((min(dx, 4 - dx) + min(dy, 4 - dy) + min(dz, 8 - dz), dx, dy, dz)
         for dx in range(4) for dy in range(4) for dz in range(8)),
        reverse=True,
    )
    xs = [lax.rem(at_chip["x"] + d, 4) for d in range(4)]
    ys = [lax.rem(at_chip["y"] + d, 4) * 32 for d in range(4)]
    zs = [lax.rem(at_chip["z"] + d, 8) * 4 for d in range(8)]
    for far, dx, dy, dz in hops:
        if far:
            pl.semaphore_signal(
                barrier, inc=1, device_id={"dp": ys[dy] + zs[dz] + xs[dx]}, device_id_type=MESH
            )
    pl.semaphore_signal(barrier, inc=1, device_id={"mp": other}, device_id_type=MESH)
    beside = [
        at_chip["y"] * 32 + at_chip["z"] * 4 + lax.rem(at_chip["x"] + d, 4) for d in (1, 2, 3)
    ]
    for chip in beside:
        pl.semaphore_signal(
            barrier, inc=1, device_id={"dp": chip, "mp": other}, device_id_type=MESH
        )

    def clear(k, _):
        rows = pl.ds(k * 16, 16)
        got[rows, CAP:8, 0:HALF] = jnp.zeros((16, 2, HALF), BF16)
        got[rows, :, HALF:] = jnp.ones((16, 8, 128), BF16)
        returned[rows, CAP:8, :] = jnp.zeros((16, 2, HALF), BF16)
        return 0

    lax.fori_loop(0, CHIPS // 16, clear, 0)

    for copy in reads[:3]:
        copy.wait()

    lab_row = labels[...]
    own_row = lax.shift_right_logical(lab_row, 10)
    own_col = as_column(own_row.astype(F32), ROWS).astype(jnp.int32)
    same = own_col == own_row
    r_i, c_i = iota((ROWS, ROWS), 0), iota((ROWS, ROWS), 1)
    rank_row = jnp.sum(jnp.where(same & (r_i < c_i), 1.0, 0.0), axis=0, keepdims=True)
    rank_col = jnp.sum(jnp.where(same & (c_i < r_i), 1.0, 0.0), axis=1, keepdims=True)
    slot_row = own_row * 8 + rank_row.astype(jnp.int32)
    slot_col = own_col * 8 + rank_col.astype(jnp.int32)
    lab_col = as_column(lab_row.astype(F32), ROWS).astype(jnp.int32)
    id_col = jnp.bitwise_and(lab_col, OWNED - 1) + 1
    at_rank = iota((ROWS, 128), 1) == rank_col.astype(jnp.int32)
    hi = jnp.where(at_rank, lax.shift_right_logical(id_col, 5).astype(F32), 0.0).astype(BF16)
    lo = jnp.where(at_rank, jnp.bitwise_and(id_col, 31).astype(F32), 0.0).astype(BF16)
    fv = feat[...]
    for k in range(OWNED // TILE):
        r = iota((TILE, ROWS), 0) + k * TILE
        pick = jnp.where(r == slot_row, 1.0, 0.0).astype(BF16)
        rows = jnp.dot(pick, fv, preferred_element_type=F32).astype(BF16)
        sent[k * 32 : (k + 1) * 32] = rows.reshape(32, 8, HALF)
        pick = jnp.where(r == own_row * 8, 1.0, 0.0).astype(BF16)
        ids = jnp.dot(pick, hi, preferred_element_type=F32) * 32.0
        ids = ids + jnp.dot(pick, lo, preferred_element_type=F32)
        sent_ids[k * 32 : (k + 1) * 32] = ids.reshape(32, 8, 128)
    c = iota((ROWS, OWNED), 1)
    route[...] = jnp.where(c == slot_col, 1.0, 0.0).astype(BF16)

    pl.semaphore_wait(barrier, CHIPS + 3)

    six = pl.ds(0, CAP)
    left = pl.ds(0, HALF)
    blocks_start(
        lambda o: sent_ids.at[o, pl.ds(0, 1)], lambda o: got_ids.at[o, pl.ds(0, 1)],
        sem.at[0], sem.at[1], me,
    )
    blocks_start(
        lambda o: sent.at[o, six], lambda o: got.at[o, six, left],
        sem.at[2], sem.at[3], me,
    )
    x = at_chip["x"]
    for chip in beside:
        for c in range(2):
            pltpu.make_async_remote_copy(
                q.at[c], qf.at[core * 4 + x], sem.at[8], sem.at[9],
                device_id={"dp": chip, "mp": c}, device_id_type=MESH,
            ).start()
    to_partner(q.at[other], qf.at[core * 4 + x], 8).start()
    home = [
        pltpu.make_async_copy(sent_ids.at[me, pl.ds(0, 1)], got_ids.at[me, pl.ds(0, 1)], sem.at[10]),
        pltpu.make_async_copy(sent.at[me, six], got.at[me, six, left], sem.at[11]),
        pltpu.make_async_copy(q.at[core], qf.at[core * 4 + x], sem.at[12]),
    ]
    for copy in home:
        copy.start()
    for copy in home:
        copy.wait()
    rest = pl.ds(0, CHIPS - 1)
    wait_recv(got_ids.at[rest, pl.ds(0, 1)], sem.at[0], sem.at[1])

    spread = jnp.broadcast_to(got_ids[:, 0:1, :], (CHIPS, 8, 128))
    here = iota((CHIPS, 8, 128), 1) == iota((CHIPS, 8, 128), 2)
    id_c = jnp.sum(jnp.where(here, spread, 0.0), axis=2, keepdims=True) - 1.0
    wide[...] = jnp.broadcast_to(id_c, (CHIPS, 8, 128)).reshape(OWNED, 128)
    id_row = jnp.transpose(wide[...])[0:1, :].astype(jnp.int32)
    wait_recv(got.at[rest, six, left], sem.at[2], sem.at[3])

    for copy in reads[3:]:
        copy.wait()
    gv = got[...].reshape(OWNED, HALF + 128)
    for k in range(OWNED // TILE):
        rows = pl.ds(k * TILE, TILE)
        hit = jnp.where(iota((TILE, OWNED), 0) + k * TILE == id_row, 1.0, 0.0).astype(BF16)
        sums = jnp.dot(hit, gv, preferred_element_type=F32)
        counts = sums[:, HALF : HALF + 1]
        old = bank[rows, :]
        mixed = 0.5 * old + 0.5 * sums[:, 0:HALF] / jnp.maximum(counts, 1.0)
        fresh = jnp.where(counts > 0, mixed, old)
        new_bank[rows, :] = fresh
        nb16[rows, :] = fresh.astype(BF16)
        count_of[rows, :] = sums[:, HALF:]

    nbv = nb16[...]
    for k in range(OWNED // TILE):
        rows = pl.ds(k * TILE, TILE)
        ids = wide[rows, :][:, 0:1].astype(jnp.int32)
        hit = jnp.where(iota((TILE, OWNED), 1) == ids, 1.0, 0.0).astype(BF16)
        near = jnp.dot(hit, nbv, preferred_element_type=F32)
        apart = got[k * 32 : (k + 1) * 32, :, 0:HALF].reshape(TILE, HALF).astype(F32) - near
        d2 = jnp.sum(apart * apart, axis=1, keepdims=True)
        d2_mine[:, k * TILE : (k + 1) * TILE] = jnp.transpose(jnp.broadcast_to(d2, (TILE, 128)))[0:8, :]
    d2x = to_partner(d2_mine, d2_theirs, 13)
    d2x.start()
    neg_row = negs[pl.ds(lax.div(me, 2), 1), :]
    want = as_column(neg_row.astype(F32), 128).astype(jnp.int32) - me * OWNED
    old_col = jnp.transpose(jnp.broadcast_to(old_conc[...], (128, OWNED)))
    conc_of[...] = old_col
    d2x.wait()

    dist = jnp.sqrt(d2_mine[0:1, :] + d2_theirs[0:1, :] + 0.25)
    for k in range(OWNED // TILE):
        rows = pl.ds(k * TILE, TILE)
        on = iota((TILE, OWNED), 0) + k * TILE == id_row
        total = jnp.sum(jnp.where(on, dist, 0.0), axis=1, keepdims=True)
        counts = count_of[rows, :][:, 0:1]
        safe = jnp.maximum(counts, 1.0)
        conc = jnp.where(counts > 0, total / (safe * jnp.log(safe + 10.0)), conc_of[rows, :][:, 0:1])
        scaled[rows, :] = (new_bank[rows, :] / conc).astype(BF16)
        conc_of[rows, :] = jnp.broadcast_to(conc, (TILE, 128))

    sv = scaled[...]
    hit = jnp.where(iota((128, OWNED), 1) == want, 1.0, 0.0).astype(BF16)
    mine[...] = jnp.dot(hit, sv, preferred_element_type=F32).astype(BF16).reshape(4, 32, HALF)
    base = lax.rem(me, 2) * 2
    swap = to_partner(mine.at[base + other], own.at[core], 21)
    swap.start()
    keep = pltpu.make_async_copy(mine.at[base + core], own.at[core], sem.at[15])
    keep.start()
    keep.wait()
    new_conc[...] = jnp.transpose(conc_of[...])[0:1, :]
    swap.wait()

    pending = []
    rounds = gather_rounds(
        own, shards.at[core], shards.at[other], core, ag_send, ag_recv, at_chip, pending
    )
    next(rounds)

    for k in range(OWNED // TILE):
        rows = pl.ds(k * TILE, TILE)
        ids = wide[rows, :][:, 0:1].astype(jnp.int32)
        hit = jnp.where(iota((TILE, OWNED), 1) == ids, 1.0, 0.0).astype(BF16)
        out = jnp.dot(hit, sv, preferred_element_type=F32).astype(BF16)
        back[k * 32 : (k + 1) * 32] = out.reshape(32, 8, HALF)
    next(rounds)
    blocks_start(
        lambda o: back.at[o, six], lambda o: returned.at[o, six],
        sem.at[4], sem.at[5], me,
    )
    copy = pltpu.make_async_copy(back.at[me, six], returned.at[me, six], sem.at[18])
    copy.start()
    copy.wait()
    for _ in rounds:
        pass

    seven = qf.at[pl.ds(0, 7)]
    wait_recv(seven, sem.at[8], sem.at[9])
    wait_send(seven, sem.at[8], sem.at[9])
    many = 2 * SHARE
    nt = (((1,), (1,)), ((), ()))
    lane = iota((many, 128), 1)
    for far in ((2, 1), (3, 0)):
        chips = [lax.rem(x + d, 4) for d in far]
        q0 = jnp.concatenate([qf[c] for c in chips], axis=0)
        q1 = jnp.concatenate([qf[4 + c] for c in chips], axis=0)
        top = jnp.full((many, 1), -3.0e38, F32)
        sums = jnp.zeros((many, 1), F32)
        for y in range(4):
            k0 = shards[:, y, :, 0].reshape(2 * TILE, HALF)
            k1 = shards[:, y, :, 1].reshape(2 * TILE, HALF)
            s = lax.dot_general(q0, k0, nt, preferred_element_type=F32)
            s = s + lax.dot_general(q1, k1, nt, preferred_element_type=F32)
            higher = jnp.maximum(top, jnp.max(s, axis=1, keepdims=True))
            shrink = jnp.exp(top - higher)
            p = jnp.exp(s - higher)
            sums = sums * shrink + jnp.sum(p, axis=1, keepdims=True)
            pb = p.astype(BF16)
            for h, kh in ((0, k0), (1, k1)):
                more = jnp.dot(pb, kh, preferred_element_type=F32)
                acc[h] = more if y == 0 else acc[h] * shrink + more
            top = higher
        both = jnp.transpose(jnp.where(lane == 0, top, sums))
        for k, c in enumerate(chips):
            stats[c] = both[0:8, k * SHARE : (k + 1) * SHARE]
            for h in range(2):
                acc16[h, c] = acc[h, k * SHARE : (k + 1) * SHARE].astype(BF16)
        for d, c in zip(far, chips):
            if d == 0:
                continue
            for h in range(2):
                to = {"dp": beside[d - 1], "mp": h}
                pltpu.make_async_remote_copy(
                    acc16.at[h, c], acc_in.at[x * 2 + core], sem.at[25], sem.at[26],
                    device_id=to, device_id_type=MESH,
                ).start()
                pltpu.make_async_remote_copy(
                    stats.at[c], stats_in.at[x * 2 + core], sem.at[27], sem.at[28],
                    device_id=to, device_id_type=MESH,
                ).start()
    to_partner(stats.at[x], stats_in.at[x * 2 + core], 27).start()
    to_partner(acc16.at[other, x], acc_in.at[x * 2 + core], 25).start()
    keep = [
        pltpu.make_async_copy(stats.at[x], stats_in.at[x * 2 + core], sem.at[29]),
        pltpu.make_async_copy(acc16.at[core, x], acc_in.at[x * 2 + core], sem.at[30]),
    ]
    for copy in keep:
        copy.start()

    wait_recv(returned.at[rest, six], sem.at[4], sem.at[5])
    pos_rows = jnp.dot(
        route[...], returned[...].reshape(OWNED, HALF), preferred_element_type=F32
    )
    part = jnp.sum(q[...].reshape(ROWS, HALF).astype(F32) * pos_rows, axis=1, keepdims=True)
    pos_mine[...] = jnp.transpose(jnp.broadcast_to(part, (ROWS, 128)))[0:8, :]
    px = to_partner(pos_mine, pos_theirs, 31)
    px.start()
    px.wait()
    positive_row = pos_mine[0:1, :] + pos_theirs[0:1, :]
    for copy in keep:
        copy.wait()
    for ref, k in ((stats_in, 27), (acc_in, 25)):
        wait_recv(ref.at[pl.ds(0, 7)], sem.at[k], sem.at[k + 1])
        wait_send(ref.at[pl.ds(0, 7)], sem.at[k], sem.at[k + 1])
    for c in range(2):
        rows = slice(c * SHARE, (c + 1) * SHARE)
        positive = positive_row[:, rows]
        tops = [stats_in[k * 2 + c, 0:1, :] for k in range(4)]
        peak = positive
        for t in tops:
            peak = jnp.maximum(peak, t)
        weights = [jnp.exp(t - peak) for t in tops]
        wp = jnp.exp(positive - peak)
        total = wp
        for k in range(4):
            total = total + stats_in[k * 2 + c, 1:2, :] * weights[k]
        loss[:, rows] = jnp.log(total) + peak - positive
        out = as_column(wp / total - 1.0, SHARE) * pos_rows[rows]
        for k in range(4):
            out = out + as_column(weights[k] / total, SHARE) * acc_in[k * 2 + c].astype(F32)
        grad[rows, :] = out

    for wait in pending:
        wait()
    wait_send(sent_ids.at[rest, pl.ds(0, 1)], sem.at[0], sem.at[1])
    wait_send(sent.at[rest, six], sem.at[2], sem.at[3])
    wait_send(back.at[rest, six], sem.at[4], sem.at[5])


def hand_out(*refs):
    copies = [pltpu.make_async_copy(refs[k], refs[4 + k], refs[8].at[k]) for k in range(4)]
    for copy in copies:
        copy.start()
    for copy in copies:
        copy.wait()


def body(features, labels, queries, bank, old_conc, neg_index):
    vmem = pl.BlockSpec(memory_space=pltpu.VMEM)
    hbm = pl.BlockSpec(memory_space=pltpu.HBM)
    outs = pl.pallas_call(
        kernel,
        out_shape=(
            jax.ShapeDtypeStruct((OWNED, HALF), F32),
            jax.ShapeDtypeStruct((1, OWNED), F32),
            jax.ShapeDtypeStruct((1, ROWS), F32),
            jax.ShapeDtypeStruct((ROWS, HALF), F32),
        ),
        in_specs=[hbm] * 6,
        out_specs=(vmem,) * 4,
        scratch_shapes=[
            pltpu.VMEM((ROWS, HALF), BF16),
            pltpu.VMEM((1, ROWS), jnp.int32),
            pltpu.VMEM((2, SHARE, HALF), BF16),
            pltpu.VMEM((OWNED, HALF), F32),
            pltpu.VMEM((1, OWNED), F32),
            pltpu.VMEM((64, 128), jnp.int32),
            pltpu.VMEM((CHIPS, 8, HALF), BF16),
            pltpu.VMEM((CHIPS, 8, 128), F32),
            pltpu.VMEM((CHIPS, 8, HALF + 128), BF16),
            pltpu.VMEM((CHIPS, 8, 128), F32),
            pltpu.VMEM((CHIPS, 8, HALF), BF16),
            pltpu.VMEM((CHIPS, 8, HALF), BF16),
            pltpu.VMEM((ROWS, OWNED), BF16),
            pltpu.VMEM((OWNED, 128), F32),
            pltpu.VMEM((8, OWNED), F32),
            pltpu.VMEM((8, OWNED), F32),
            pltpu.VMEM((OWNED, HALF), BF16),
            pltpu.VMEM((OWNED, HALF), BF16),
            pltpu.VMEM((OWNED, 128), F32),
            pltpu.VMEM((OWNED, 128), F32),
            pltpu.VMEM((4, 32, HALF), BF16),
            pltpu.VMEM((2, 32, HALF), BF16),
            pltpu.VMEM((2, 4, 8, 2, 32, HALF), BF16),
            pltpu.VMEM((8, SHARE, HALF), BF16),
            pltpu.VMEM((2, 2 * SHARE, HALF), F32),
            pltpu.VMEM((2, 4, SHARE, HALF), BF16),
            pltpu.VMEM((8, SHARE, HALF), BF16),
            pltpu.VMEM((4, 8, SHARE), F32),
            pltpu.VMEM((8, 8, SHARE), F32),
            pltpu.VMEM((8, ROWS), F32),
            pltpu.VMEM((8, ROWS), F32),
            pltpu.SemaphoreType.DMA((96,)),
            pltpu.SemaphoreType.DMA((96,)),
            pltpu.SemaphoreType.DMA((40,)),
        ],
        compiler_params=pltpu.CompilerParams(
            collective_id=0, has_side_effects=True, vmem_limit_bytes=32 << 20
        ),
        name="step",
    )(
        *(
            pltpu.with_memory_space_constraint(a, pltpu.HBM)
            for a in (
                features,
                labels.reshape(1, ROWS),
                queries.reshape(2, SHARE, HALF),
                bank,
                old_conc.reshape(1, OWNED),
                neg_index.reshape(64, 128),
            )
        )
    )
    new_bank, new_conc, loss, grad = pl.pallas_call(
        hand_out,
        out_shape=tuple(jax.ShapeDtypeStruct(o.shape, o.dtype) for o in outs),
        in_specs=[vmem] * 4,
        out_specs=(hbm,) * 4,
        scratch_shapes=[pltpu.SemaphoreType.DMA((4,))],
        compiler_params=pltpu.CompilerParams(vmem_limit_bytes=4 << 20),
        name="hand_out",
    )(*outs)
    return new_bank, new_conc.reshape(OWNED), loss.reshape(ROWS), grad


def solution(mesh):
    return jax.shard_map(
        body,
        mesh=mesh,
        in_specs=(P("dp", "mp"), P("dp"), P("dp", "mp"), P("dp", "mp"), P("dp"), P()),
        out_specs=(P("dp", "mp"), P("dp"), P("dp"), P("dp", "mp")),
        check_vma=False,
    )
```

```python
import functools
import jax
import jax.numpy as jnp
from jax import lax
from jax.experimental import pallas as pl
from jax.experimental.pallas import tpu as pltpu
from jax.sharding import PartitionSpec as P

MESH = pl.DeviceIdType.MESH
F32, BF16 = jnp.float32, jnp.bfloat16
LEN = {"x": 4, "y": 4, "z": 8}
CHIPS = 128
OWNED = 1024
ROWS = 256
HALF = 384
CAP = 6
SHARE = 128
TILE = 256


def iota(shape, dim):
    return lax.broadcasted_iota(jnp.int32, shape, dim)


def peer(me, d):
    return lax.rem(me + d, CHIPS)


def blocks_start(src, dst, ssem, rsem, me, low=1, high=CHIPS):
    def go(d, _):
        o = peer(me, d)
        pltpu.make_async_remote_copy(
            src(o), dst(me), ssem, rsem, device_id={"dp": o}, device_id_type=MESH
        ).start()
        return 0

    lax.fori_loop(low, high, go, 0)


def wait_send(ref, ssem, rsem):
    pltpu.make_async_remote_copy(
        ref, ref, ssem, rsem, device_id={"dp": 0}, device_id_type=MESH
    ).wait_send()


def wait_recv(ref, ssem, rsem):
    pltpu.make_async_remote_copy(
        ref, ref, ssem, rsem, device_id={"dp": 0}, device_id_type=MESH
    ).wait_recv()


def gather_rounds(mine, gathered, theirs, core, ssem, rsem, at_chip, pending, handed):
    count = [0]
    lengths = {"y": LEN["y"], "z": LEN["z"]}

    def off(axis, k):
        return lax.rem(at_chip[axis] + k + lengths[axis], lengths[axis])

    def chip(axis, k):
        d = dict(at_chip)
        d[axis] = off(axis, k)
        return (d["y"] * 8 + d["z"]) * 4 + d["x"]

    def send(src, dst, **to):
        i = count[0]
        count[0] += 1
        copy = pltpu.make_async_remote_copy(
            src, dst, ssem.at[i], rsem.at[i], device_id=to, device_id_type=MESH
        )
        copy.start()
        pending.append(copy.wait_send)
        return i

    def arrived(ref, i):
        wait_recv(ref, ssem.at[i], rsem.at[i])

    def at(y, z, half=None, ref=gathered):
        ref = ref.at[off("y", y), off("z", z)]
        return ref if half is None else ref.at[half]

    def hand_over(y, z):
        i = send(at(y, z), at(y, z), mp=1 - core)
        handed.append((y, lambda: arrived(at(y, z, ref=theirs), i)))

    flying = {}

    def along_y(z, src=None):
        src = at(0, z) if src is None else src
        flying[z] = (send(src, at(0, z), dp=chip("y", 1)), send(src, at(0, z), dp=chip("y", -1)))

    def on_y(z):
        arrived(at(-1, z), flying[z][0])
        right = send(at(-1, z, 0), at(-1, z, 0), dp=chip("y", 1))
        arrived(at(1, z), flying[z][1])
        flying[z] = (right, send(at(1, z, 1), at(1, z, 1), dp=chip("y", -1)))
        hand_over(-1, z)
        hand_over(1, z)

    def end_y(z):
        arrived(at(2, z, 0), flying[z][0])
        arrived(at(2, z, 1), flying[z][1])
        hand_over(2, z)

    up, down = chip("z", 1), chip("z", -1)
    from_down, from_up = send(mine, at(0, 0), dp=up), send(mine, at(0, 0), dp=down)
    along_y(0, mine)
    i = count[0]
    count[0] += 1
    local = pltpu.make_async_copy(mine, at(0, 0), ssem.at[i])
    local.start()
    local.wait()
    hand_over(0, 0)
    yield
    for s in (1, 2, 3):
        part = (0, 1) if s == 3 else (None, None)
        arrived(at(0, -s), from_down)
        from_down = send(at(0, -s, part[0]), at(0, -s, part[0]), dp=up)
        arrived(at(0, s), from_up)
        from_up = send(at(0, s, part[1]), at(0, s, part[1]), dp=down)
        along_y(-s)
        along_y(s)
        hand_over(0, -s)
        hand_over(0, s)
        for z in ((0,), (-1, 1), (-2, 2))[s - 1]:
            on_y(z)
        yield
    arrived(at(0, 4, 0), from_down)
    arrived(at(0, 4, 1), from_up)
    along_y(4)
    hand_over(0, 4)
    yield
    for z in (-3, 3):
        on_y(z)
    end_y(0)
    yield
    on_y(4)
    for z in (-1, 1):
        end_y(z)
    yield
    for z in (-2, 2, -3, 3, 4):
        end_y(z)


def as_column(row, n):
    eye = iota((n, n), 0) == iota((n, n), 1)
    return jnp.sum(jnp.where(eye, row, jnp.zeros_like(row)), axis=1, keepdims=True)


def kernel(
    feat_in, labels_in, q_in, bank_in, old_conc_in, negs_in,
    new_bank, new_conc, loss, grad,
    feat, labels, q, bank, old_conc, negs,
    sent, sent_ids, got, got_ids, back, returned, route, wide,
    d2_mine, d2_theirs, nb16, scaled, count_of, conc_of, mine, own,
    shards, qf, acc, acc16, acc_in, stats, stats_in, pos_mine, pos_theirs,
    ag_send, ag_recv, sem,
):
    me = lax.axis_index("dp")
    core = lax.axis_index("mp")
    other = 1 - core
    at_chip = {
        "x": lax.rem(me, 4),
        "y": lax.div(me, 32),
        "z": lax.rem(lax.div(me, 4), 8),
    }

    def to_partner(src, dst, k):
        return pltpu.make_async_remote_copy(
            src, dst, sem.at[k], sem.at[k + 1], device_id={"mp": other}, device_id_type=MESH
        )

    reads = [
        pltpu.make_async_copy(src, dst, sem.at[k])
        for src, dst, k in (
            (labels_in, labels, 33), (feat_in, feat, 34), (q_in, q, 35),
            (old_conc_in, old_conc, 36), (negs_in, negs, 37), (bank_in, bank, 38),
        )
    ]
    for copy in reads:
        copy.start()

    barrier = pltpu.get_barrier_semaphore()

    hops = sorted(
        ((min(dx, 4 - dx) + min(dy, 4 - dy) + min(dz, 8 - dz), dx, dy, dz)
         for dx in range(4) for dy in range(4) for dz in range(8)),
        reverse=True,
    )
    xs = [lax.rem(at_chip["x"] + d, 4) for d in range(4)]
    ys = [lax.rem(at_chip["y"] + d, 4) * 32 for d in range(4)]
    zs = [lax.rem(at_chip["z"] + d, 8) * 4 for d in range(8)]
    for far, dx, dy, dz in hops:
        if far:
            pl.semaphore_signal(
                barrier, inc=1, device_id={"dp": ys[dy] + zs[dz] + xs[dx]}, device_id_type=MESH
            )
    pl.semaphore_signal(barrier, inc=1, device_id={"mp": other}, device_id_type=MESH)
    beside = [
        at_chip["y"] * 32 + at_chip["z"] * 4 + lax.rem(at_chip["x"] + d, 4) for d in (1, 2, 3)
    ]
    for chip in beside:
        pl.semaphore_signal(
            barrier, inc=1, device_id={"dp": chip, "mp": other}, device_id_type=MESH
        )

    def clear(k, _):
        rows = pl.ds(k * 16, 16)
        got[rows, CAP:8, 0:HALF] = jnp.zeros((16, 2, HALF), BF16)
        got[rows, :, HALF:] = jnp.ones((16, 8, 128), BF16)
        returned[rows, CAP:8, :] = jnp.zeros((16, 2, HALF), BF16)
        return 0

    lax.fori_loop(0, CHIPS // 16, clear, 0)

    for copy in reads[:3]:
        copy.wait()

    lab_row = labels[...]
    own_row = lax.shift_right_logical(lab_row, 10)
    own_col = as_column(own_row.astype(F32), ROWS).astype(jnp.int32)
    same = own_col == own_row
    r_i, c_i = iota((ROWS, ROWS), 0), iota((ROWS, ROWS), 1)
    rank_row = jnp.sum(jnp.where(same & (r_i < c_i), 1.0, 0.0), axis=0, keepdims=True)
    rank_col = jnp.sum(jnp.where(same & (c_i < r_i), 1.0, 0.0), axis=1, keepdims=True)
    slot_row = own_row * 8 + rank_row.astype(jnp.int32)
    slot_col = own_col * 8 + rank_col.astype(jnp.int32)
    lab_col = as_column(lab_row.astype(F32), ROWS).astype(jnp.int32)
    id_col = jnp.bitwise_and(lab_col, OWNED - 1) + 1
    at_rank = iota((ROWS, 128), 1) == rank_col.astype(jnp.int32)
    hi = jnp.where(at_rank, lax.shift_right_logical(id_col, 5).astype(F32), 0.0).astype(BF16)
    lo = jnp.where(at_rank, jnp.bitwise_and(id_col, 31).astype(F32), 0.0).astype(BF16)
    fv = feat[...]
    for k in range(OWNED // TILE):
        r = iota((TILE, ROWS), 0) + k * TILE
        pick = jnp.where(r == slot_row, 1.0, 0.0).astype(BF16)
        rows = jnp.dot(pick, fv, preferred_element_type=F32).astype(BF16)
        sent[k * 32 : (k + 1) * 32] = rows.reshape(32, 8, HALF)
        pick = jnp.where(r == own_row * 8, 1.0, 0.0).astype(BF16)
        ids = jnp.dot(pick, hi, preferred_element_type=F32) * 32.0
        ids = ids + jnp.dot(pick, lo, preferred_element_type=F32)
        sent_ids[k * 32 : (k + 1) * 32] = ids.reshape(32, 8, 128)
    c = iota((ROWS, OWNED), 1)
    route[...] = jnp.where(c == slot_col, 1.0, 0.0).astype(BF16)

    pl.semaphore_wait(barrier, CHIPS + 3)

    six = pl.ds(0, CAP)
    left = pl.ds(0, HALF)
    blocks_start(
        lambda o: sent_ids.at[o, pl.ds(0, 1)], lambda o: got_ids.at[o, pl.ds(0, 1)],
        sem.at[0], sem.at[1], me,
    )
    blocks_start(
        lambda o: sent.at[o, six], lambda o: got.at[o, six, left],
        sem.at[2], sem.at[3], me,
    )
    x = at_chip["x"]
    for chip in beside:
        for c in range(2):
            pltpu.make_async_remote_copy(
                q.at[c], qf.at[core * 4 + x], sem.at[8], sem.at[9],
                device_id={"dp": chip, "mp": c}, device_id_type=MESH,
            ).start()
    to_partner(q.at[other], qf.at[core * 4 + x], 8).start()
    home = [
        pltpu.make_async_copy(sent_ids.at[me, pl.ds(0, 1)], got_ids.at[me, pl.ds(0, 1)], sem.at[10]),
        pltpu.make_async_copy(sent.at[me, six], got.at[me, six, left], sem.at[11]),
        pltpu.make_async_copy(q.at[core], qf.at[core * 4 + x], sem.at[12]),
    ]
    for copy in home:
        copy.start()
    for copy in home:
        copy.wait()
    rest = pl.ds(0, CHIPS - 1)
    wait_recv(got_ids.at[rest, pl.ds(0, 1)], sem.at[0], sem.at[1])

    spread = jnp.broadcast_to(got_ids[:, 0:1, :], (CHIPS, 8, 128))
    here = iota((CHIPS, 8, 128), 1) == iota((CHIPS, 8, 128), 2)
    id_c = jnp.sum(jnp.where(here, spread, 0.0), axis=2, keepdims=True) - 1.0
    wide[...] = jnp.broadcast_to(id_c, (CHIPS, 8, 128)).reshape(OWNED, 128)
    id_row = jnp.transpose(wide[...])[0:1, :].astype(jnp.int32)
    wait_recv(got.at[rest, six, left], sem.at[2], sem.at[3])

    for copy in reads[3:]:
        copy.wait()
    gv = got[...].reshape(OWNED, HALF + 128)
    for k in range(OWNED // TILE):
        rows = pl.ds(k * TILE, TILE)
        hit = jnp.where(iota((TILE, OWNED), 0) + k * TILE == id_row, 1.0, 0.0).astype(BF16)
        sums = jnp.dot(hit, gv, preferred_element_type=F32)
        counts = sums[:, HALF : HALF + 1]
        old = bank[rows, :]
        mixed = 0.5 * old + 0.5 * sums[:, 0:HALF] / jnp.maximum(counts, 1.0)
        fresh = jnp.where(counts > 0, mixed, old)
        new_bank[rows, :] = fresh
        nb16[rows, :] = fresh.astype(BF16)
        count_of[rows, :] = sums[:, HALF:]

    nbv = nb16[...]
    for k in range(OWNED // TILE):
        rows = pl.ds(k * TILE, TILE)
        ids = wide[rows, :][:, 0:1].astype(jnp.int32)
        hit = jnp.where(iota((TILE, OWNED), 1) == ids, 1.0, 0.0).astype(BF16)
        near = jnp.dot(hit, nbv, preferred_element_type=F32)
        apart = got[k * 32 : (k + 1) * 32, :, 0:HALF].reshape(TILE, HALF).astype(F32) - near
        d2 = jnp.sum(apart * apart, axis=1, keepdims=True)
        d2_mine[:, k * TILE : (k + 1) * TILE] = jnp.transpose(jnp.broadcast_to(d2, (TILE, 128)))[0:8, :]
    d2x = to_partner(d2_mine, d2_theirs, 13)
    d2x.start()
    neg_row = negs[pl.ds(lax.div(me, 2), 1), :]
    want = as_column(neg_row.astype(F32), 128).astype(jnp.int32) - me * OWNED
    old_col = jnp.transpose(jnp.broadcast_to(old_conc[...], (128, OWNED)))
    conc_of[...] = old_col
    d2x.wait()

    dist = jnp.sqrt(d2_mine[0:1, :] + d2_theirs[0:1, :] + 0.25)
    for k in range(OWNED // TILE):
        rows = pl.ds(k * TILE, TILE)
        on = iota((TILE, OWNED), 0) + k * TILE == id_row
        total = jnp.sum(jnp.where(on, dist, 0.0), axis=1, keepdims=True)
        counts = count_of[rows, :][:, 0:1]
        safe = jnp.maximum(counts, 1.0)
        conc = jnp.where(counts > 0, total / (safe * jnp.log(safe + 10.0)), conc_of[rows, :][:, 0:1])
        scaled[rows, :] = (new_bank[rows, :] / conc).astype(BF16)
        conc_of[rows, :] = jnp.broadcast_to(conc, (TILE, 128))

    sv = scaled[...]
    hit = jnp.where(iota((128, OWNED), 1) == want, 1.0, 0.0).astype(BF16)
    mine[...] = jnp.dot(hit, sv, preferred_element_type=F32).astype(BF16).reshape(4, 32, HALF)
    base = lax.rem(me, 2) * 2
    swap = to_partner(mine.at[base + other], own.at[core], 21)
    swap.start()
    keep = pltpu.make_async_copy(mine.at[base + core], own.at[core], sem.at[15])
    keep.start()
    keep.wait()
    new_conc[...] = jnp.transpose(conc_of[...])[0:1, :]
    swap.wait()

    pending = []
    handed = []
    rounds = gather_rounds(
        own, shards.at[core], shards.at[other], core, ag_send, ag_recv, at_chip, pending, handed
    )
    next(rounds)

    for k in range(OWNED // TILE):
        rows = pl.ds(k * TILE, TILE)
        ids = wide[rows, :][:, 0:1].astype(jnp.int32)
        hit = jnp.where(iota((TILE, OWNED), 1) == ids, 1.0, 0.0).astype(BF16)
        out = jnp.dot(hit, sv, preferred_element_type=F32).astype(BF16)
        back[k * 32 : (k + 1) * 32] = out.reshape(32, 8, HALF)
    copy = pltpu.make_async_copy(back.at[me, six], returned.at[me, six], sem.at[18])
    copy.start()
    copy.wait()

    def give_back(low, high):
        blocks_start(
            lambda o: back.at[o, six], lambda o: returned.at[o, six],
            sem.at[4], sem.at[5], me, low, high,
        )

    many = 2 * SHARE
    nt = (((1,), (1,)), ((), ()))
    parts = ((2, 1), (3, 0))
    tops, totals = [None, None], [None, None]

    def attend(y):
        for plane, wait in handed:
            if plane == y:
                wait()
        there = pl.ds(lax.rem(at_chip["y"] + y + 4, 4), 1)
        k0 = shards[:, there, :, 0].reshape(2 * TILE, HALF)
        k1 = shards[:, there, :, 1].reshape(2 * TILE, HALF)
        for n, far in enumerate(parts):
            chips = [lax.rem(x + d, 4) for d in far]
            q0 = jnp.concatenate([qf[c] for c in chips], axis=0)
            q1 = jnp.concatenate([qf[4 + c] for c in chips], axis=0)
            s = lax.dot_general(q0, k0, nt, preferred_element_type=F32)
            s = s + lax.dot_general(q1, k1, nt, preferred_element_type=F32)
            high = jnp.max(s, axis=1, keepdims=True)
            if tops[n] is not None:
                high = jnp.maximum(tops[n], high)
                shrink = jnp.exp(tops[n] - high)
            p = jnp.exp(s - high)
            total = jnp.sum(p, axis=1, keepdims=True)
            pb = p.astype(BF16)
            for h, kh in ((0, k0), (1, k1)):
                more = jnp.dot(pb, kh, preferred_element_type=F32)
                acc[n, h] = more if tops[n] is None else acc[n, h] * shrink + more
            totals[n] = total if tops[n] is None else totals[n] * shrink + total
            tops[n] = high
            if y == 2:
                send_part(n, chips)

    def send_part(n, chips):
        both = jnp.transpose(jnp.where(iota((many, 128), 1) == 0, tops[n], totals[n]))
        for k, (d, c) in enumerate(zip(parts[n], chips)):
            stats[c] = both[0:8, k * SHARE : (k + 1) * SHARE]
            for h in range(2):
                acc16[h, c] = acc[n, h, k * SHARE : (k + 1) * SHARE].astype(BF16)
        for d, c in zip(parts[n], chips):
            if d == 0:
                continue
            for h in range(2):
                to = {"dp": beside[d - 1], "mp": h}
                pltpu.make_async_remote_copy(
                    acc16.at[h, c], acc_in.at[x * 2 + core], sem.at[25], sem.at[26],
                    device_id=to, device_id_type=MESH,
                ).start()
                pltpu.make_async_remote_copy(
                    stats.at[c], stats_in.at[x * 2 + core], sem.at[27], sem.at[28],
                    device_id=to, device_id_type=MESH,
                ).start()

    for _ in range(4):
        next(rounds)
    give_back(1, 44)
    next(rounds)
    seven = qf.at[pl.ds(0, 7)]
    wait_recv(seven, sem.at[8], sem.at[9])
    wait_send(seven, sem.at[8], sem.at[9])
    give_back(44, 86)
    attend(0)
    next(rounds)
    give_back(86, CHIPS)
    attend(-1)
    attend(1)
    for _ in rounds:
        pass
    attend(2)
    to_partner(stats.at[x], stats_in.at[x * 2 + core], 27).start()
    to_partner(acc16.at[other, x], acc_in.at[x * 2 + core], 25).start()
    keep = [
        pltpu.make_async_copy(stats.at[x], stats_in.at[x * 2 + core], sem.at[29]),
        pltpu.make_async_copy(acc16.at[core, x], acc_in.at[x * 2 + core], sem.at[30]),
    ]
    for copy in keep:
        copy.start()

    wait_recv(returned.at[rest, six], sem.at[4], sem.at[5])
    pos_rows = jnp.dot(
        route[...], returned[...].reshape(OWNED, HALF), preferred_element_type=F32
    )
    part = jnp.sum(q[...].reshape(ROWS, HALF).astype(F32) * pos_rows, axis=1, keepdims=True)
    pos_mine[...] = jnp.transpose(jnp.broadcast_to(part, (ROWS, 128)))[0:8, :]
    px = to_partner(pos_mine, pos_theirs, 31)
    px.start()
    px.wait()
    positive_row = pos_mine[0:1, :] + pos_theirs[0:1, :]
    for copy in keep:
        copy.wait()
    for ref, k in ((stats_in, 27), (acc_in, 25)):
        wait_recv(ref.at[pl.ds(0, 7)], sem.at[k], sem.at[k + 1])
        wait_send(ref.at[pl.ds(0, 7)], sem.at[k], sem.at[k + 1])
    for c in range(2):
        rows = slice(c * SHARE, (c + 1) * SHARE)
        positive = positive_row[:, rows]
        tops = [stats_in[k * 2 + c, 0:1, :] for k in range(4)]
        peak = positive
        for t in tops:
            peak = jnp.maximum(peak, t)
        weights = [jnp.exp(t - peak) for t in tops]
        wp = jnp.exp(positive - peak)
        total = wp
        for k in range(4):
            total = total + stats_in[k * 2 + c, 1:2, :] * weights[k]
        loss[:, rows] = jnp.log(total) + peak - positive
        out = as_column(wp / total - 1.0, SHARE) * pos_rows[rows]
        for k in range(4):
            out = out + as_column(weights[k] / total, SHARE) * acc_in[k * 2 + c].astype(F32)
        grad[rows, :] = out

    for wait in pending:
        wait()
    wait_send(sent_ids.at[rest, pl.ds(0, 1)], sem.at[0], sem.at[1])
    wait_send(sent.at[rest, six], sem.at[2], sem.at[3])
    wait_send(back.at[rest, six], sem.at[4], sem.at[5])


def hand_out(*refs):
    copies = [pltpu.make_async_copy(refs[k], refs[4 + k], refs[8].at[k]) for k in range(4)]
    for copy in copies:
        copy.start()
    for copy in copies:
        copy.wait()


def body(features, labels, queries, bank, old_conc, neg_index):
    vmem = pl.BlockSpec(memory_space=pltpu.VMEM)
    hbm = pl.BlockSpec(memory_space=pltpu.HBM)
    outs = pl.pallas_call(
        kernel,
        out_shape=(
            jax.ShapeDtypeStruct((OWNED, HALF), F32),
            jax.ShapeDtypeStruct((1, OWNED), F32),
            jax.ShapeDtypeStruct((1, ROWS), F32),
            jax.ShapeDtypeStruct((ROWS, HALF), F32),
        ),
        in_specs=[hbm] * 6,
        out_specs=(vmem,) * 4,
        scratch_shapes=[
            pltpu.VMEM((ROWS, HALF), BF16),
            pltpu.VMEM((1, ROWS), jnp.int32),
            pltpu.VMEM((2, SHARE, HALF), BF16),
            pltpu.VMEM((OWNED, HALF), F32),
            pltpu.VMEM((1, OWNED), F32),
            pltpu.VMEM((64, 128), jnp.int32),
            pltpu.VMEM((CHIPS, 8, HALF), BF16),
            pltpu.VMEM((CHIPS, 8, 128), F32),
            pltpu.VMEM((CHIPS, 8, HALF + 128), BF16),
            pltpu.VMEM((CHIPS, 8, 128), F32),
            pltpu.VMEM((CHIPS, 8, HALF), BF16),
            pltpu.VMEM((CHIPS, 8, HALF), BF16),
            pltpu.VMEM((ROWS, OWNED), BF16),
            pltpu.VMEM((OWNED, 128), F32),
            pltpu.VMEM((8, OWNED), F32),
            pltpu.VMEM((8, OWNED), F32),
            pltpu.VMEM((OWNED, HALF), BF16),
            pltpu.VMEM((OWNED, HALF), BF16),
            pltpu.VMEM((OWNED, 128), F32),
            pltpu.VMEM((OWNED, 128), F32),
            pltpu.VMEM((4, 32, HALF), BF16),
            pltpu.VMEM((2, 32, HALF), BF16),
            pltpu.VMEM((2, 4, 8, 2, 32, HALF), BF16),
            pltpu.VMEM((8, SHARE, HALF), BF16),
            pltpu.VMEM((2, 2, 2 * SHARE, HALF), F32),
            pltpu.VMEM((2, 4, SHARE, HALF), BF16),
            pltpu.VMEM((8, SHARE, HALF), BF16),
            pltpu.VMEM((4, 8, SHARE), F32),
            pltpu.VMEM((8, 8, SHARE), F32),
            pltpu.VMEM((8, ROWS), F32),
            pltpu.VMEM((8, ROWS), F32),
            pltpu.SemaphoreType.DMA((96,)),
            pltpu.SemaphoreType.DMA((96,)),
            pltpu.SemaphoreType.DMA((40,)),
        ],
        compiler_params=pltpu.CompilerParams(
            collective_id=0, has_side_effects=True, vmem_limit_bytes=32 << 20
        ),
        name="step",
    )(
        *(
            pltpu.with_memory_space_constraint(a, pltpu.HBM)
            for a in (
                features,
                labels.reshape(1, ROWS),
                queries.reshape(2, SHARE, HALF),
                bank,
                old_conc.reshape(1, OWNED),
                neg_index.reshape(64, 128),
            )
        )
    )
    new_bank, new_conc, loss, grad = pl.pallas_call(
        hand_out,
        out_shape=tuple(jax.ShapeDtypeStruct(o.shape, o.dtype) for o in outs),
        in_specs=[vmem] * 4,
        out_specs=(hbm,) * 4,
        scratch_shapes=[pltpu.SemaphoreType.DMA((4,))],
        compiler_params=pltpu.CompilerParams(vmem_limit_bytes=4 << 20),
        name="hand_out",
    )(*outs)
    return new_bank, new_conc.reshape(OWNED), loss.reshape(ROWS), grad


def solution(mesh):
    return jax.shard_map(
        body,
        mesh=mesh,
        in_specs=(P("dp", "mp"), P("dp"), P("dp", "mp"), P("dp", "mp"), P("dp"), P()),
        out_specs=(P("dp", "mp"), P("dp"), P("dp"), P("dp", "mp")),
        check_vma=False,
    )
```

```python
import functools
import jax
import jax.numpy as jnp
from jax import lax
from jax.experimental import pallas as pl
from jax.experimental.pallas import tpu as pltpu
from jax.sharding import PartitionSpec as P

MESH = pl.DeviceIdType.MESH
F32, BF16 = jnp.float32, jnp.bfloat16
LEN = {"x": 4, "y": 4, "z": 8}
CHIPS = 128
OWNED = 1024
ROWS = 256
HALF = 384
CAP = 6
SHARE = 128
TILE = 256


def iota(shape, dim):
    return lax.broadcasted_iota(jnp.int32, shape, dim)


def peer(me, d):
    return lax.rem(me + d, CHIPS)


def blocks_start(src, dst, ssem, rsem, me, low=1, high=CHIPS):
    def go(d, _):
        o = peer(me, d)
        pltpu.make_async_remote_copy(
            src(o), dst(me), ssem, rsem, device_id={"dp": o}, device_id_type=MESH
        ).start()
        return 0

    lax.fori_loop(low, high, go, 0)


def wait_send(ref, ssem, rsem):
    pltpu.make_async_remote_copy(
        ref, ref, ssem, rsem, device_id={"dp": 0}, device_id_type=MESH
    ).wait_send()


def wait_recv(ref, ssem, rsem):
    pltpu.make_async_remote_copy(
        ref, ref, ssem, rsem, device_id={"dp": 0}, device_id_type=MESH
    ).wait_recv()


def gather_rounds(mine, gathered, theirs, core, ssem, rsem, at_chip, pending, handed):
    count = [0]
    lengths = {"y": LEN["y"], "z": LEN["z"]}

    def off(axis, k):
        return lax.rem(at_chip[axis] + k + lengths[axis], lengths[axis])

    def chip(axis, k):
        d = dict(at_chip)
        d[axis] = off(axis, k)
        return (d["y"] * 8 + d["z"]) * 4 + d["x"]

    def send(src, dst, **to):
        i = count[0]
        count[0] += 1
        copy = pltpu.make_async_remote_copy(
            src, dst, ssem.at[i], rsem.at[i], device_id=to, device_id_type=MESH
        )
        copy.start()
        pending.append(copy.wait_send)
        return i

    def arrived(ref, i):
        wait_recv(ref, ssem.at[i], rsem.at[i])

    def at(y, z, half=None, ref=gathered):
        ref = ref.at[off("y", y), off("z", z)]
        return ref if half is None else ref.at[half]

    def hand_over(y, z):
        i = send(at(y, z), at(y, z), mp=1 - core)
        handed.append((y, lambda: arrived(at(y, z, ref=theirs), i)))

    flying = {}

    def along_y(z, src=None):
        src = at(0, z) if src is None else src
        flying[z] = (send(src, at(0, z), dp=chip("y", 1)), send(src, at(0, z), dp=chip("y", -1)))

    def on_y(z):
        arrived(at(-1, z), flying[z][0])
        right = send(at(-1, z, 0), at(-1, z, 0), dp=chip("y", 1))
        arrived(at(1, z), flying[z][1])
        flying[z] = (right, send(at(1, z, 1), at(1, z, 1), dp=chip("y", -1)))
        hand_over(-1, z)
        hand_over(1, z)

    def end_y(z):
        arrived(at(2, z, 0), flying[z][0])
        arrived(at(2, z, 1), flying[z][1])
        hand_over(2, z)

    up, down = chip("z", 1), chip("z", -1)
    from_down, from_up = send(mine, at(0, 0), dp=up), send(mine, at(0, 0), dp=down)
    along_y(0, mine)
    i = count[0]
    count[0] += 1
    local = pltpu.make_async_copy(mine, at(0, 0), ssem.at[i])
    local.start()
    local.wait()
    hand_over(0, 0)
    yield
    for s in (1, 2, 3):
        part = (0, 1) if s == 3 else (None, None)
        arrived(at(0, -s), from_down)
        from_down = send(at(0, -s, part[0]), at(0, -s, part[0]), dp=up)
        arrived(at(0, s), from_up)
        from_up = send(at(0, s, part[1]), at(0, s, part[1]), dp=down)
        along_y(-s)
        along_y(s)
        hand_over(0, -s)
        hand_over(0, s)
        for z in ((0,), (-1, 1), (-2, 2))[s - 1]:
            on_y(z)
        yield
    arrived(at(0, 4, 0), from_down)
    arrived(at(0, 4, 1), from_up)
    along_y(4)
    hand_over(0, 4)
    yield
    for z in (-3, 3):
        on_y(z)
    end_y(0)
    yield
    on_y(4)
    for z in (-1, 1):
        end_y(z)
    yield
    for z in (-2, 2, -3, 3, 4):
        end_y(z)


def as_column(row, n):
    eye = iota((n, n), 0) == iota((n, n), 1)
    return jnp.sum(jnp.where(eye, row, jnp.zeros_like(row)), axis=1, keepdims=True)


def kernel(
    feat_in, labels_in, q_in, bank_in, old_conc_in, negs_in,
    new_bank, new_conc, loss, grad,
    feat, labels, q, bank, old_conc, negs,
    sent, sent_ids, got, got_ids, back, returned, route, wide,
    d2_mine, d2_theirs, nb16, scaled, count_of, conc_of, mine, own,
    shards, qf, acc, acc16, acc_in, stats, stats_in, pos_mine, pos_theirs,
    ag_send, ag_recv, sem,
):
    me = lax.axis_index("dp")
    core = lax.axis_index("mp")
    other = 1 - core
    at_chip = {
        "x": lax.rem(me, 4),
        "y": lax.div(me, 32),
        "z": lax.rem(lax.div(me, 4), 8),
    }

    def to_partner(src, dst, k):
        return pltpu.make_async_remote_copy(
            src, dst, sem.at[k], sem.at[k + 1], device_id={"mp": other}, device_id_type=MESH
        )

    reads = [
        pltpu.make_async_copy(src, dst, sem.at[k])
        for src, dst, k in (
            (labels_in, labels, 33), (feat_in, feat, 34), (q_in, q, 35),
            (old_conc_in, old_conc, 36), (negs_in, negs, 37), (bank_in, bank, 38),
        )
    ]
    for copy in reads:
        copy.start()

    barrier = pltpu.get_barrier_semaphore()

    hops = sorted(
        ((min(dx, 4 - dx) + min(dy, 4 - dy) + min(dz, 8 - dz), dx, dy, dz)
         for dx in range(4) for dy in range(4) for dz in range(8)),
        reverse=True,
    )
    xs = [lax.rem(at_chip["x"] + d, 4) for d in range(4)]
    ys = [lax.rem(at_chip["y"] + d, 4) * 32 for d in range(4)]
    zs = [lax.rem(at_chip["z"] + d, 8) * 4 for d in range(8)]
    for far, dx, dy, dz in hops:
        if far:
            pl.semaphore_signal(
                barrier, inc=1, device_id={"dp": ys[dy] + zs[dz] + xs[dx]}, device_id_type=MESH
            )
    pl.semaphore_signal(barrier, inc=1, device_id={"mp": other}, device_id_type=MESH)
    beside = [
        at_chip["y"] * 32 + at_chip["z"] * 4 + lax.rem(at_chip["x"] + d, 4) for d in (1, 2, 3)
    ]
    for chip in beside:
        pl.semaphore_signal(
            barrier, inc=1, device_id={"dp": chip, "mp": other}, device_id_type=MESH
        )

    def clear(k, _):
        rows = pl.ds(k * 16, 16)
        got[rows, CAP:8, 0:HALF] = jnp.zeros((16, 2, HALF), BF16)
        got[rows, :, HALF:] = jnp.ones((16, 8, 128), BF16)
        returned[rows, CAP:8, :] = jnp.zeros((16, 2, HALF), BF16)
        return 0

    lax.fori_loop(0, CHIPS // 16, clear, 0)

    for copy in reads[:3]:
        copy.wait()

    lab_row = labels[...]
    own_row = lax.shift_right_logical(lab_row, 10)
    own_col = as_column(own_row.astype(F32), ROWS).astype(jnp.int32)
    same = own_col == own_row
    r_i, c_i = iota((ROWS, ROWS), 0), iota((ROWS, ROWS), 1)
    rank_row = jnp.sum(jnp.where(same & (r_i < c_i), 1.0, 0.0), axis=0, keepdims=True)
    rank_col = jnp.sum(jnp.where(same & (c_i < r_i), 1.0, 0.0), axis=1, keepdims=True)
    slot_row = own_row * 8 + rank_row.astype(jnp.int32)
    slot_col = own_col * 8 + rank_col.astype(jnp.int32)
    lab_col = as_column(lab_row.astype(F32), ROWS).astype(jnp.int32)
    id_col = jnp.bitwise_and(lab_col, OWNED - 1) + 1
    at_rank = iota((ROWS, 128), 1) == rank_col.astype(jnp.int32)
    hi = jnp.where(at_rank, lax.shift_right_logical(id_col, 5).astype(F32), 0.0).astype(BF16)
    lo = jnp.where(at_rank, jnp.bitwise_and(id_col, 31).astype(F32), 0.0).astype(BF16)
    fv = feat[...]
    for k in range(OWNED // TILE):
        r = iota((TILE, ROWS), 0) + k * TILE
        pick = jnp.where(r == slot_row, 1.0, 0.0).astype(BF16)
        rows = jnp.dot(pick, fv, preferred_element_type=F32).astype(BF16)
        sent[k * 32 : (k + 1) * 32] = rows.reshape(32, 8, HALF)
        pick = jnp.where(r == own_row * 8, 1.0, 0.0).astype(BF16)
        ids = jnp.dot(pick, hi, preferred_element_type=F32) * 32.0
        ids = ids + jnp.dot(pick, lo, preferred_element_type=F32)
        sent_ids[k * 32 : (k + 1) * 32] = ids.reshape(32, 8, 128)
    c = iota((ROWS, OWNED), 1)
    route[...] = jnp.where(c == slot_col, 1.0, 0.0).astype(BF16)

    pl.semaphore_wait(barrier, CHIPS + 3)

    six = pl.ds(0, CAP)
    left = pl.ds(0, HALF)
    blocks_start(
        lambda o: sent_ids.at[o, pl.ds(0, 1)], lambda o: got_ids.at[o, pl.ds(0, 1)],
        sem.at[0], sem.at[1], me,
    )
    blocks_start(
        lambda o: sent.at[o, six], lambda o: got.at[o, six, left],
        sem.at[2], sem.at[3], me,
    )
    home = [
        pltpu.make_async_copy(sent_ids.at[me, pl.ds(0, 1)], got_ids.at[me, pl.ds(0, 1)], sem.at[10]),
        pltpu.make_async_copy(sent.at[me, six], got.at[me, six, left], sem.at[11]),
    ]
    for copy in home:
        copy.start()
    for copy in home:
        copy.wait()
    rest = pl.ds(0, CHIPS - 1)
    wait_recv(got_ids.at[rest, pl.ds(0, 1)], sem.at[0], sem.at[1])

    spread = jnp.broadcast_to(got_ids[:, 0:1, :], (CHIPS, 8, 128))
    here = iota((CHIPS, 8, 128), 1) == iota((CHIPS, 8, 128), 2)
    id_c = jnp.sum(jnp.where(here, spread, 0.0), axis=2, keepdims=True) - 1.0
    wide[...] = jnp.broadcast_to(id_c, (CHIPS, 8, 128)).reshape(OWNED, 128)
    id_row = jnp.transpose(wide[...])[0:1, :].astype(jnp.int32)
    wait_recv(got.at[rest, six, left], sem.at[2], sem.at[3])

    x = at_chip["x"]
    for chip in beside:
        for c in range(2):
            pltpu.make_async_remote_copy(
                q.at[c], qf.at[core * 4 + x], sem.at[8], sem.at[9],
                device_id={"dp": chip, "mp": c}, device_id_type=MESH,
            ).start()
    to_partner(q.at[other], qf.at[core * 4 + x], 8).start()
    stay = pltpu.make_async_copy(q.at[core], qf.at[core * 4 + x], sem.at[12])
    stay.start()

    for copy in reads[3:]:
        copy.wait()
    gv = got[...].reshape(OWNED, HALF + 128)
    for k in range(OWNED // TILE):
        rows = pl.ds(k * TILE, TILE)
        hit = jnp.where(iota((TILE, OWNED), 0) + k * TILE == id_row, 1.0, 0.0).astype(BF16)
        sums = jnp.dot(hit, gv, preferred_element_type=F32)
        counts = sums[:, HALF : HALF + 1]
        old = bank[rows, :]
        mixed = 0.5 * old + 0.5 * sums[:, 0:HALF] / jnp.maximum(counts, 1.0)
        fresh = jnp.where(counts > 0, mixed, old)
        new_bank[rows, :] = fresh
        nb16[rows, :] = fresh.astype(BF16)
        count_of[rows, :] = sums[:, HALF:]

    nbv = nb16[...]
    for k in range(OWNED // TILE):
        rows = pl.ds(k * TILE, TILE)
        ids = wide[rows, :][:, 0:1].astype(jnp.int32)
        hit = jnp.where(iota((TILE, OWNED), 1) == ids, 1.0, 0.0).astype(BF16)
        near = jnp.dot(hit, nbv, preferred_element_type=F32)
        apart = got[k * 32 : (k + 1) * 32, :, 0:HALF].reshape(TILE, HALF).astype(F32) - near
        d2 = jnp.sum(apart * apart, axis=1, keepdims=True)
        d2_mine[:, k * TILE : (k + 1) * TILE] = jnp.transpose(jnp.broadcast_to(d2, (TILE, 128)))[0:8, :]
    d2x = to_partner(d2_mine, d2_theirs, 13)
    d2x.start()
    neg_row = negs[pl.ds(lax.div(me, 2), 1), :]
    want = as_column(neg_row.astype(F32), 128).astype(jnp.int32) - me * OWNED
    old_col = jnp.transpose(jnp.broadcast_to(old_conc[...], (128, OWNED)))
    conc_of[...] = old_col
    d2x.wait()

    dist = jnp.sqrt(d2_mine[0:1, :] + d2_theirs[0:1, :] + 0.25)
    for k in range(OWNED // TILE):
        rows = pl.ds(k * TILE, TILE)
        on = iota((TILE, OWNED), 0) + k * TILE == id_row
        total = jnp.sum(jnp.where(on, dist, 0.0), axis=1, keepdims=True)
        counts = count_of[rows, :][:, 0:1]
        safe = jnp.maximum(counts, 1.0)
        conc = jnp.where(counts > 0, total / (safe * jnp.log(safe + 10.0)), conc_of[rows, :][:, 0:1])
        scaled[rows, :] = (new_bank[rows, :] / conc).astype(BF16)
        conc_of[rows, :] = jnp.broadcast_to(conc, (TILE, 128))

    sv = scaled[...]
    hit = jnp.where(iota((128, OWNED), 1) == want, 1.0, 0.0).astype(BF16)
    mine[...] = jnp.dot(hit, sv, preferred_element_type=F32).astype(BF16).reshape(4, 32, HALF)
    base = lax.rem(me, 2) * 2
    swap = to_partner(mine.at[base + other], own.at[core], 21)
    swap.start()
    keep = pltpu.make_async_copy(mine.at[base + core], own.at[core], sem.at[15])
    keep.start()
    keep.wait()
    new_conc[...] = jnp.transpose(conc_of[...])[0:1, :]
    swap.wait()

    pending = []
    handed = []
    rounds = gather_rounds(
        own, shards.at[core], shards.at[other], core, ag_send, ag_recv, at_chip, pending, handed
    )
    next(rounds)

    for k in range(OWNED // TILE):
        rows = pl.ds(k * TILE, TILE)
        ids = wide[rows, :][:, 0:1].astype(jnp.int32)
        hit = jnp.where(iota((TILE, OWNED), 1) == ids, 1.0, 0.0).astype(BF16)
        out = jnp.dot(hit, sv, preferred_element_type=F32).astype(BF16)
        back[k * 32 : (k + 1) * 32] = out.reshape(32, 8, HALF)
    copy = pltpu.make_async_copy(back.at[me, six], returned.at[me, six], sem.at[18])
    copy.start()
    copy.wait()

    def give_back(low, high):
        blocks_start(
            lambda o: back.at[o, six], lambda o: returned.at[o, six],
            sem.at[4], sem.at[5], me, low, high,
        )

    many = 2 * SHARE
    nt = (((1,), (1,)), ((), ()))
    parts = ((2, 1), (3, 0))
    tops, totals = [None, None], [None, None]

    def attend(y):
        for plane, wait in handed:
            if plane == y:
                wait()
        there = pl.ds(lax.rem(at_chip["y"] + y + 4, 4), 1)
        k0 = shards[:, there, :, 0].reshape(2 * TILE, HALF)
        k1 = shards[:, there, :, 1].reshape(2 * TILE, HALF)
        for n, far in enumerate(parts):
            chips = [lax.rem(x + d, 4) for d in far]
            q0 = jnp.concatenate([qf[c] for c in chips], axis=0)
            q1 = jnp.concatenate([qf[4 + c] for c in chips], axis=0)
            s = lax.dot_general(q0, k0, nt, preferred_element_type=F32)
            s = s + lax.dot_general(q1, k1, nt, preferred_element_type=F32)
            high = jnp.max(s, axis=1, keepdims=True)
            if tops[n] is not None:
                high = jnp.maximum(tops[n], high)
                shrink = jnp.exp(tops[n] - high)
            p = jnp.exp(s - high)
            total = jnp.sum(p, axis=1, keepdims=True)
            pb = p.astype(BF16)
            for h, kh in ((0, k0), (1, k1)):
                more = jnp.dot(pb, kh, preferred_element_type=F32)
                acc[n, h] = more if tops[n] is None else acc[n, h] * shrink + more
            totals[n] = total if tops[n] is None else totals[n] * shrink + total
            tops[n] = high
            if y == 2:
                send_part(n, chips)

    def send_part(n, chips):
        both = jnp.transpose(jnp.where(iota((many, 128), 1) == 0, tops[n], totals[n]))
        for k, (d, c) in enumerate(zip(parts[n], chips)):
            stats[c] = both[0:8, k * SHARE : (k + 1) * SHARE]
            for h in range(2):
                acc16[h, c] = acc[n, h, k * SHARE : (k + 1) * SHARE].astype(BF16)
        for d, c in zip(parts[n], chips):
            if d == 0:
                continue
            for h in range(2):
                to = {"dp": beside[d - 1], "mp": h}
                pltpu.make_async_remote_copy(
                    acc16.at[h, c], acc_in.at[x * 2 + core], sem.at[25], sem.at[26],
                    device_id=to, device_id_type=MESH,
                ).start()
                pltpu.make_async_remote_copy(
                    stats.at[c], stats_in.at[x * 2 + core], sem.at[27], sem.at[28],
                    device_id=to, device_id_type=MESH,
                ).start()

    for low in (1, 15, 29):
        next(rounds)
        give_back(low, low + 14)
    next(rounds)
    give_back(43, 71)
    next(rounds)
    seven = qf.at[pl.ds(0, 7)]
    wait_recv(seven, sem.at[8], sem.at[9])
    wait_send(seven, sem.at[8], sem.at[9])
    stay.wait()
    give_back(71, 99)
    attend(0)
    next(rounds)
    give_back(99, CHIPS)
    attend(-1)
    attend(1)
    for _ in rounds:
        pass
    attend(2)
    to_partner(stats.at[x], stats_in.at[x * 2 + core], 27).start()
    to_partner(acc16.at[other, x], acc_in.at[x * 2 + core], 25).start()
    keep = [
        pltpu.make_async_copy(stats.at[x], stats_in.at[x * 2 + core], sem.at[29]),
        pltpu.make_async_copy(acc16.at[core, x], acc_in.at[x * 2 + core], sem.at[30]),
    ]
    for copy in keep:
        copy.start()

    wait_recv(returned.at[rest, six], sem.at[4], sem.at[5])
    pos_rows = jnp.dot(
        route[...], returned[...].reshape(OWNED, HALF), preferred_element_type=F32
    )
    part = jnp.sum(q[...].reshape(ROWS, HALF).astype(F32) * pos_rows, axis=1, keepdims=True)
    pos_mine[...] = jnp.transpose(jnp.broadcast_to(part, (ROWS, 128)))[0:8, :]
    px = to_partner(pos_mine, pos_theirs, 31)
    px.start()
    px.wait()
    positive_row = pos_mine[0:1, :] + pos_theirs[0:1, :]
    for copy in keep:
        copy.wait()
    for ref, k in ((stats_in, 27), (acc_in, 25)):
        wait_recv(ref.at[pl.ds(0, 7)], sem.at[k], sem.at[k + 1])
        wait_send(ref.at[pl.ds(0, 7)], sem.at[k], sem.at[k + 1])
    for c in range(2):
        rows = slice(c * SHARE, (c + 1) * SHARE)
        positive = positive_row[:, rows]
        tops = [stats_in[k * 2 + c, 0:1, :] for k in range(4)]
        peak = positive
        for t in tops:
            peak = jnp.maximum(peak, t)
        weights = [jnp.exp(t - peak) for t in tops]
        wp = jnp.exp(positive - peak)
        total = wp
        for k in range(4):
            total = total + stats_in[k * 2 + c, 1:2, :] * weights[k]
        loss[:, rows] = jnp.log(total) + peak - positive
        out = as_column(wp / total - 1.0, SHARE) * pos_rows[rows]
        for k in range(4):
            out = out + as_column(weights[k] / total, SHARE) * acc_in[k * 2 + c].astype(F32)
        grad[rows, :] = out

    for wait in pending:
        wait()
    wait_send(sent_ids.at[rest, pl.ds(0, 1)], sem.at[0], sem.at[1])
    wait_send(sent.at[rest, six], sem.at[2], sem.at[3])
    wait_send(back.at[rest, six], sem.at[4], sem.at[5])


def hand_out(*refs):
    copies = [pltpu.make_async_copy(refs[k], refs[4 + k], refs[8].at[k]) for k in range(4)]
    for copy in copies:
        copy.start()
    for copy in copies:
        copy.wait()


def body(features, labels, queries, bank, old_conc, neg_index):
    vmem = pl.BlockSpec(memory_space=pltpu.VMEM)
    hbm = pl.BlockSpec(memory_space=pltpu.HBM)
    outs = pl.pallas_call(
        kernel,
        out_shape=(
            jax.ShapeDtypeStruct((OWNED, HALF), F32),
            jax.ShapeDtypeStruct((1, OWNED), F32),
            jax.ShapeDtypeStruct((1, ROWS), F32),
            jax.ShapeDtypeStruct((ROWS, HALF), F32),
        ),
        in_specs=[hbm] * 6,
        out_specs=(vmem,) * 4,
        scratch_shapes=[
            pltpu.VMEM((ROWS, HALF), BF16),
            pltpu.VMEM((1, ROWS), jnp.int32),
            pltpu.VMEM((2, SHARE, HALF), BF16),
            pltpu.VMEM((OWNED, HALF), F32),
            pltpu.VMEM((1, OWNED), F32),
            pltpu.VMEM((64, 128), jnp.int32),
            pltpu.VMEM((CHIPS, 8, HALF), BF16),
            pltpu.VMEM((CHIPS, 8, 128), F32),
            pltpu.VMEM((CHIPS, 8, HALF + 128), BF16),
            pltpu.VMEM((CHIPS, 8, 128), F32),
            pltpu.VMEM((CHIPS, 8, HALF), BF16),
            pltpu.VMEM((CHIPS, 8, HALF), BF16),
            pltpu.VMEM((ROWS, OWNED), BF16),
            pltpu.VMEM((OWNED, 128), F32),
            pltpu.VMEM((8, OWNED), F32),
            pltpu.VMEM((8, OWNED), F32),
            pltpu.VMEM((OWNED, HALF), BF16),
            pltpu.VMEM((OWNED, HALF), BF16),
            pltpu.VMEM((OWNED, 128), F32),
            pltpu.VMEM((OWNED, 128), F32),
            pltpu.VMEM((4, 32, HALF), BF16),
            pltpu.VMEM((2, 32, HALF), BF16),
            pltpu.VMEM((2, 4, 8, 2, 32, HALF), BF16),
            pltpu.VMEM((8, SHARE, HALF), BF16),
            pltpu.VMEM((2, 2, 2 * SHARE, HALF), F32),
            pltpu.VMEM((2, 4, SHARE, HALF), BF16),
            pltpu.VMEM((8, SHARE, HALF), BF16),
            pltpu.VMEM((4, 8, SHARE), F32),
            pltpu.VMEM((8, 8, SHARE), F32),
            pltpu.VMEM((8, ROWS), F32),
            pltpu.VMEM((8, ROWS), F32),
            pltpu.SemaphoreType.DMA((96,)),
            pltpu.SemaphoreType.DMA((96,)),
            pltpu.SemaphoreType.DMA((40,)),
        ],
        compiler_params=pltpu.CompilerParams(
            collective_id=0, has_side_effects=True, vmem_limit_bytes=32 << 20
        ),
        name="step",
    )(
        *(
            pltpu.with_memory_space_constraint(a, pltpu.HBM)
            for a in (
                features,
                labels.reshape(1, ROWS),
                queries.reshape(2, SHARE, HALF),
                bank,
                old_conc.reshape(1, OWNED),
                neg_index.reshape(64, 128),
            )
        )
    )
    new_bank, new_conc, loss, grad = pl.pallas_call(
        hand_out,
        out_shape=tuple(jax.ShapeDtypeStruct(o.shape, o.dtype) for o in outs),
        in_specs=[vmem] * 4,
        out_specs=(hbm,) * 4,
        scratch_shapes=[pltpu.SemaphoreType.DMA((4,))],
        compiler_params=pltpu.CompilerParams(vmem_limit_bytes=4 << 20),
        name="hand_out",
    )(*outs)
    return new_bank, new_conc.reshape(OWNED), loss.reshape(ROWS), grad


def solution(mesh):
    return jax.shard_map(
        body,
        mesh=mesh,
        in_specs=(P("dp", "mp"), P("dp"), P("dp", "mp"), P("dp", "mp"), P("dp"), P()),
        out_specs=(P("dp", "mp"), P("dp"), P("dp"), P("dp", "mp")),
        check_vma=False,
    )
```

```python
import functools
import jax
import jax.numpy as jnp
from jax import lax
from jax.experimental import pallas as pl
from jax.experimental.pallas import tpu as pltpu
from jax.sharding import PartitionSpec as P

MESH = pl.DeviceIdType.MESH
F32, BF16 = jnp.float32, jnp.bfloat16
LEN = {"x": 4, "y": 4, "z": 8}
CHIPS = 128
OWNED = 1024
ROWS = 256
HALF = 384
CAP = 6
SHARE = 128
TILE = 256


def iota(shape, dim):
    return lax.broadcasted_iota(jnp.int32, shape, dim)


def peer(me, d):
    return lax.rem(me + d, CHIPS)


def blocks_start(src, dst, ssem, rsem, me, low=1, high=CHIPS):
    def go(d, _):
        o = peer(me, d)
        pltpu.make_async_remote_copy(
            src(o), dst(me), ssem, rsem, device_id={"dp": o}, device_id_type=MESH
        ).start()
        return 0

    lax.fori_loop(low, high, go, 0)


def wait_send(ref, ssem, rsem):
    pltpu.make_async_remote_copy(
        ref, ref, ssem, rsem, device_id={"dp": 0}, device_id_type=MESH
    ).wait_send()


def wait_recv(ref, ssem, rsem):
    pltpu.make_async_remote_copy(
        ref, ref, ssem, rsem, device_id={"dp": 0}, device_id_type=MESH
    ).wait_recv()


def gather_rounds(mine, gathered, theirs, core, ssem, rsem, at_chip, pending, handed):
    count = [0]
    lengths = {"y": LEN["y"], "z": LEN["z"]}

    def off(axis, k):
        return lax.rem(at_chip[axis] + k + lengths[axis], lengths[axis])

    def chip(axis, k):
        d = dict(at_chip)
        d[axis] = off(axis, k)
        return (d["y"] * 8 + d["z"]) * 4 + d["x"]

    def send(src, dst, **to):
        i = count[0]
        count[0] += 1
        copy = pltpu.make_async_remote_copy(
            src, dst, ssem.at[i], rsem.at[i], device_id=to, device_id_type=MESH
        )
        copy.start()
        pending.append(copy.wait_send)
        return i

    def arrived(ref, i):
        wait_recv(ref, ssem.at[i], rsem.at[i])

    def at(y, z, half=None, ref=gathered):
        ref = ref.at[off("y", y), off("z", z)]
        return ref if half is None else ref.at[half]

    def hand_over(y, z=None):
        mine, its = (r.at[off("y", y)] if z is None else at(y, z, ref=r) for r in (gathered, theirs))
        i = send(mine, mine, mp=1 - core)
        handed.append((y, lambda: arrived(its, i)))

    flying = {}

    def along_y(z, src=None):
        src = at(0, z) if src is None else src
        flying[z] = (send(src, at(0, z), dp=chip("y", 1)), send(src, at(0, z), dp=chip("y", -1)))

    def on_y(z):
        arrived(at(-1, z), flying[z][0])
        right = send(at(-1, z, 0), at(-1, z, 0), dp=chip("y", 1))
        arrived(at(1, z), flying[z][1])
        flying[z] = (right, send(at(1, z, 1), at(1, z, 1), dp=chip("y", -1)))

    def end_y(z):
        arrived(at(2, z, 0), flying[z][0])
        arrived(at(2, z, 1), flying[z][1])
        hand_over(2, z)

    up, down = chip("z", 1), chip("z", -1)
    from_down, from_up = send(mine, at(0, 0), dp=up), send(mine, at(0, 0), dp=down)
    along_y(0, mine)
    i = count[0]
    count[0] += 1
    local = pltpu.make_async_copy(mine, at(0, 0), ssem.at[i])
    local.start()
    local.wait()
    yield
    for s in (1, 2, 3):
        part = (0, 1) if s == 3 else (None, None)
        arrived(at(0, -s), from_down)
        from_down = send(at(0, -s, part[0]), at(0, -s, part[0]), dp=up)
        arrived(at(0, s), from_up)
        from_up = send(at(0, s, part[1]), at(0, s, part[1]), dp=down)
        along_y(-s)
        along_y(s)
        for z in ((0,), (-1, 1), (-2, 2))[s - 1]:
            on_y(z)
        yield
    arrived(at(0, 4, 0), from_down)
    arrived(at(0, 4, 1), from_up)
    along_y(4)
    hand_over(0)
    yield
    for z in (-3, 3):
        on_y(z)
    end_y(0)
    yield
    on_y(4)
    hand_over(-1)
    hand_over(1)
    for z in (-1, 1):
        end_y(z)
    yield
    for z in (-2, 2, -3, 3, 4):
        end_y(z)


def as_column(row, n):
    eye = iota((n, n), 0) == iota((n, n), 1)
    return jnp.sum(jnp.where(eye, row, jnp.zeros_like(row)), axis=1, keepdims=True)


def kernel(
    feat_in, labels_in, q_in, bank_in, old_conc_in, negs_in,
    new_bank, new_conc, loss, grad,
    feat, labels, q, bank, old_conc, negs,
    sent, sent_ids, got, got_ids, back, returned, route, wide,
    d2_mine, d2_theirs, nb16, scaled, count_of, conc_of, mine,
    shards, qf, acc, acc16, acc_in, stats, stats_in, pos_mine, pos_theirs,
    ag_send, ag_recv, sem,
):
    me = lax.axis_index("dp")
    core = lax.axis_index("mp")
    other = 1 - core
    at_chip = {
        "x": lax.rem(me, 4),
        "y": lax.div(me, 32),
        "z": lax.rem(lax.div(me, 4), 8),
    }

    def to_partner(src, dst, k):
        return pltpu.make_async_remote_copy(
            src, dst, sem.at[k], sem.at[k + 1], device_id={"mp": other}, device_id_type=MESH
        )

    reads = [
        pltpu.make_async_copy(src, dst, sem.at[k])
        for src, dst, k in (
            (labels_in, labels, 33), (feat_in, feat, 34), (q_in, q, 35),
            (old_conc_in, old_conc, 36), (negs_in, negs, 37), (bank_in, bank, 38),
        )
    ]
    for copy in reads:
        copy.start()

    barrier = pltpu.get_barrier_semaphore()

    hops = sorted(
        ((min(dx, 4 - dx) + min(dy, 4 - dy) + min(dz, 8 - dz), dx, dy, dz)
         for dx in range(4) for dy in range(4) for dz in range(8)),
        reverse=True,
    )
    xs = [lax.rem(at_chip["x"] + d, 4) for d in range(4)]
    ys = [lax.rem(at_chip["y"] + d, 4) * 32 for d in range(4)]
    zs = [lax.rem(at_chip["z"] + d, 8) * 4 for d in range(8)]
    for far, dx, dy, dz in hops:
        if far:
            pl.semaphore_signal(
                barrier, inc=1, device_id={"dp": ys[dy] + zs[dz] + xs[dx]}, device_id_type=MESH
            )
    pl.semaphore_signal(barrier, inc=1, device_id={"mp": other}, device_id_type=MESH)
    beside = [
        at_chip["y"] * 32 + at_chip["z"] * 4 + lax.rem(at_chip["x"] + d, 4) for d in (1, 2, 3)
    ]
    for chip in beside:
        pl.semaphore_signal(
            barrier, inc=1, device_id={"dp": chip, "mp": other}, device_id_type=MESH
        )

    def clear(k, _):
        rows = pl.ds(k * 16, 16)
        got[rows, CAP:8, 0:HALF] = jnp.zeros((16, 2, HALF), BF16)
        got[rows, :, HALF:] = jnp.ones((16, 8, 128), BF16)
        returned[rows, CAP:8, :] = jnp.zeros((16, 2, HALF), BF16)
        return 0

    lax.fori_loop(0, CHIPS // 16, clear, 0)

    for copy in reads[:3]:
        copy.wait()

    lab_row = labels[...]
    own_row = lax.shift_right_logical(lab_row, 10)
    own_col = as_column(own_row.astype(F32), ROWS).astype(jnp.int32)
    same = own_col == own_row
    r_i, c_i = iota((ROWS, ROWS), 0), iota((ROWS, ROWS), 1)
    rank_row = jnp.sum(jnp.where(same & (r_i < c_i), 1.0, 0.0), axis=0, keepdims=True)
    rank_col = jnp.sum(jnp.where(same & (c_i < r_i), 1.0, 0.0), axis=1, keepdims=True)
    slot_row = own_row * 8 + rank_row.astype(jnp.int32)
    slot_col = own_col * 8 + rank_col.astype(jnp.int32)
    lab_col = as_column(lab_row.astype(F32), ROWS).astype(jnp.int32)
    id_col = jnp.bitwise_and(lab_col, OWNED - 1) + 1
    at_rank = iota((ROWS, 128), 1) == rank_col.astype(jnp.int32)
    hi = jnp.where(at_rank, lax.shift_right_logical(id_col, 5).astype(F32), 0.0).astype(BF16)
    lo = jnp.where(at_rank, jnp.bitwise_and(id_col, 31).astype(F32), 0.0).astype(BF16)
    fv = feat[...]
    for k in range(OWNED // TILE):
        r = iota((TILE, ROWS), 0) + k * TILE
        pick = jnp.where(r == slot_row, 1.0, 0.0).astype(BF16)
        rows = jnp.dot(pick, fv, preferred_element_type=F32).astype(BF16)
        sent[k * 32 : (k + 1) * 32] = rows.reshape(32, 8, HALF)
        pick = jnp.where(r == own_row * 8, 1.0, 0.0).astype(BF16)
        ids = jnp.dot(pick, hi, preferred_element_type=F32) * 32.0
        ids = ids + jnp.dot(pick, lo, preferred_element_type=F32)
        sent_ids[k * 32 : (k + 1) * 32] = ids.reshape(32, 8, 128)
    c = iota((ROWS, OWNED), 1)
    route[...] = jnp.where(c == slot_col, 1.0, 0.0).astype(BF16)

    pl.semaphore_wait(barrier, CHIPS + 3)

    six = pl.ds(0, CAP)
    left = pl.ds(0, HALF)
    blocks_start(
        lambda o: sent_ids.at[o, pl.ds(0, 1)], lambda o: got_ids.at[o, pl.ds(0, 1)],
        sem.at[0], sem.at[1], me,
    )
    blocks_start(
        lambda o: sent.at[o, six], lambda o: got.at[o, six, left],
        sem.at[2], sem.at[3], me,
    )
    home = [
        pltpu.make_async_copy(sent_ids.at[me, pl.ds(0, 1)], got_ids.at[me, pl.ds(0, 1)], sem.at[10]),
        pltpu.make_async_copy(sent.at[me, six], got.at[me, six, left], sem.at[11]),
    ]
    for copy in home:
        copy.start()
    for copy in home:
        copy.wait()
    rest = pl.ds(0, CHIPS - 1)
    wait_recv(got_ids.at[rest, pl.ds(0, 1)], sem.at[0], sem.at[1])

    spread = jnp.broadcast_to(got_ids[:, 0:1, :], (CHIPS, 8, 128))
    here = iota((CHIPS, 8, 128), 1) == iota((CHIPS, 8, 128), 2)
    id_c = jnp.sum(jnp.where(here, spread, 0.0), axis=2, keepdims=True) - 1.0
    wide[...] = jnp.broadcast_to(id_c, (CHIPS, 8, 128)).reshape(OWNED, 128)
    id_row = jnp.transpose(wide[...])[0:1, :].astype(jnp.int32)
    wait_recv(got.at[rest, six, left], sem.at[2], sem.at[3])

    x = at_chip["x"]
    for chip in beside:
        for c in range(2):
            pltpu.make_async_remote_copy(
                q.at[c], qf.at[core * 4 + x], sem.at[8], sem.at[9],
                device_id={"dp": chip, "mp": c}, device_id_type=MESH,
            ).start()
    to_partner(q.at[other], qf.at[core * 4 + x], 8).start()
    stay = pltpu.make_async_copy(q.at[core], qf.at[core * 4 + x], sem.at[12])
    stay.start()

    for copy in reads[3:]:
        copy.wait()
    gv = got[...].reshape(OWNED, HALF + 128)
    for k in range(OWNED // TILE):
        rows = pl.ds(k * TILE, TILE)
        hit = jnp.where(iota((TILE, OWNED), 0) + k * TILE == id_row, 1.0, 0.0).astype(BF16)
        sums = jnp.dot(hit, gv, preferred_element_type=F32)
        counts = sums[:, HALF : HALF + 1]
        old = bank[rows, :]
        mixed = 0.5 * old + 0.5 * sums[:, 0:HALF] / jnp.maximum(counts, 1.0)
        fresh = jnp.where(counts > 0, mixed, old)
        new_bank[rows, :] = fresh
        nb16[rows, :] = fresh.astype(BF16)
        count_of[rows, :] = sums[:, HALF:]

    nbv = nb16[...]
    for k in range(OWNED // TILE):
        rows = pl.ds(k * TILE, TILE)
        ids = wide[rows, :][:, 0:1].astype(jnp.int32)
        hit = jnp.where(iota((TILE, OWNED), 1) == ids, 1.0, 0.0).astype(BF16)
        near = jnp.dot(hit, nbv, preferred_element_type=F32)
        apart = got[k * 32 : (k + 1) * 32, :, 0:HALF].reshape(TILE, HALF).astype(F32) - near
        d2 = jnp.sum(apart * apart, axis=1, keepdims=True)
        d2_mine[:, k * TILE : (k + 1) * TILE] = jnp.transpose(jnp.broadcast_to(d2, (TILE, 128)))[0:8, :]
    d2x = to_partner(d2_mine, d2_theirs, 13)
    d2x.start()
    neg_row = negs[pl.ds(lax.div(me, 2), 1), :]
    want = as_column(neg_row.astype(F32), 128).astype(jnp.int32) - me * OWNED
    old_col = jnp.transpose(jnp.broadcast_to(old_conc[...], (128, OWNED)))
    conc_of[...] = old_col
    d2x.wait()

    dist = jnp.sqrt(d2_mine[0:1, :] + d2_theirs[0:1, :] + 0.25)
    for k in range(OWNED // TILE):
        rows = pl.ds(k * TILE, TILE)
        on = iota((TILE, OWNED), 0) + k * TILE == id_row
        total = jnp.sum(jnp.where(on, dist, 0.0), axis=1, keepdims=True)
        counts = count_of[rows, :][:, 0:1]
        safe = jnp.maximum(counts, 1.0)
        conc = jnp.where(counts > 0, total / (safe * jnp.log(safe + 10.0)), conc_of[rows, :][:, 0:1])
        scaled[rows, :] = (new_bank[rows, :] / conc).astype(BF16)
        conc_of[rows, :] = jnp.broadcast_to(conc, (TILE, 128))

    sv = scaled[...]
    hit = jnp.where(iota((128, OWNED), 1) == want, 1.0, 0.0).astype(BF16)
    mine[...] = jnp.dot(hit, sv, preferred_element_type=F32).astype(BF16).reshape(2, 2, 32, HALF)
    pending = []
    handed = []
    rounds = gather_rounds(
        mine.at[lax.rem(me, 2)], shards.at[core], shards.at[other], core,
        ag_send, ag_recv, at_chip, pending, handed,
    )
    next(rounds)
    new_conc[...] = jnp.transpose(conc_of[...])[0:1, :]

    for k in range(OWNED // TILE):
        rows = pl.ds(k * TILE, TILE)
        ids = wide[rows, :][:, 0:1].astype(jnp.int32)
        hit = jnp.where(iota((TILE, OWNED), 1) == ids, 1.0, 0.0).astype(BF16)
        out = jnp.dot(hit, sv, preferred_element_type=F32).astype(BF16)
        back[k * 32 : (k + 1) * 32] = out.reshape(32, 8, HALF)
    copy = pltpu.make_async_copy(back.at[me, six], returned.at[me, six], sem.at[18])
    copy.start()
    copy.wait()

    def give_back(low, high):
        blocks_start(
            lambda o: back.at[o, six], lambda o: returned.at[o, six],
            sem.at[4], sem.at[5], me, low, high,
        )

    many = 2 * SHARE
    nt = (((1,), (1,)), ((), ()))
    parts = ((2, 1), (3, 0))
    tops, totals = [None, None], [None, None]

    def attend(y):
        for plane, wait in handed:
            if plane == y:
                wait()
        there = pl.ds(lax.rem(at_chip["y"] + y + 4, 4), 1)
        k0 = shards[0, there].reshape(2 * TILE, HALF)
        k1 = shards[1, there].reshape(2 * TILE, HALF)
        for n, far in enumerate(parts):
            chips = [lax.rem(x + d, 4) for d in far]
            q0 = jnp.concatenate([qf[c] for c in chips], axis=0)
            q1 = jnp.concatenate([qf[4 + c] for c in chips], axis=0)
            s = lax.dot_general(q0, k0, nt, preferred_element_type=F32)
            s = s + lax.dot_general(q1, k1, nt, preferred_element_type=F32)
            high = jnp.max(s, axis=1, keepdims=True)
            if tops[n] is not None:
                high = jnp.maximum(tops[n], high)
                shrink = jnp.exp(tops[n] - high)
            p = jnp.exp(s - high)
            total = jnp.sum(p, axis=1, keepdims=True)
            pb = p.astype(BF16)
            for h, kh in ((0, k0), (1, k1)):
                more = jnp.dot(pb, kh, preferred_element_type=F32)
                acc[n, h] = more if tops[n] is None else acc[n, h] * shrink + more
            totals[n] = total if tops[n] is None else totals[n] * shrink + total
            tops[n] = high
            if y == 2:
                send_part(n, chips)

    def send_part(n, chips):
        both = jnp.transpose(jnp.where(iota((many, 128), 1) == 0, tops[n], totals[n]))
        for k, (d, c) in enumerate(zip(parts[n], chips)):
            stats[c] = both[0:8, k * SHARE : (k + 1) * SHARE]
            for h in range(2):
                acc16[h, c] = acc[n, h, k * SHARE : (k + 1) * SHARE].astype(BF16)
        for d, c in zip(parts[n], chips):
            if d == 0:
                continue
            for h in range(2):
                to = {"dp": beside[d - 1], "mp": h}
                pltpu.make_async_remote_copy(
                    acc16.at[h, c], acc_in.at[x * 2 + core], sem.at[25], sem.at[26],
                    device_id=to, device_id_type=MESH,
                ).start()
                pltpu.make_async_remote_copy(
                    stats.at[c], stats_in.at[x * 2 + core], sem.at[27], sem.at[28],
                    device_id=to, device_id_type=MESH,
                ).start()

    for _ in range(4):
        next(rounds)
    give_back(1, 44)
    next(rounds)
    seven = qf.at[pl.ds(0, 7)]
    wait_recv(seven, sem.at[8], sem.at[9])
    wait_send(seven, sem.at[8], sem.at[9])
    stay.wait()
    give_back(44, 86)
    attend(0)
    next(rounds)
    give_back(86, CHIPS)
    attend(-1)
    attend(1)
    for _ in rounds:
        pass
    attend(2)
    to_partner(stats.at[x], stats_in.at[x * 2 + core], 27).start()
    to_partner(acc16.at[other, x], acc_in.at[x * 2 + core], 25).start()
    keep = [
        pltpu.make_async_copy(stats.at[x], stats_in.at[x * 2 + core], sem.at[29]),
        pltpu.make_async_copy(acc16.at[core, x], acc_in.at[x * 2 + core], sem.at[30]),
    ]
    for copy in keep:
        copy.start()

    wait_recv(returned.at[rest, six], sem.at[4], sem.at[5])
    pos_rows = jnp.dot(
        route[...], returned[...].reshape(OWNED, HALF), preferred_element_type=F32
    )
    part = jnp.sum(q[...].reshape(ROWS, HALF).astype(F32) * pos_rows, axis=1, keepdims=True)
    pos_mine[...] = jnp.transpose(jnp.broadcast_to(part, (ROWS, 128)))[0:8, :]
    px = to_partner(pos_mine, pos_theirs, 31)
    px.start()
    px.wait()
    positive_row = pos_mine[0:1, :] + pos_theirs[0:1, :]
    for copy in keep:
        copy.wait()
    for ref, k in ((stats_in, 27), (acc_in, 25)):
        wait_recv(ref.at[pl.ds(0, 7)], sem.at[k], sem.at[k + 1])
        wait_send(ref.at[pl.ds(0, 7)], sem.at[k], sem.at[k + 1])
    for c in range(2):
        rows = slice(c * SHARE, (c + 1) * SHARE)
        positive = positive_row[:, rows]
        tops = [stats_in[k * 2 + c, 0:1, :] for k in range(4)]
        peak = positive
        for t in tops:
            peak = jnp.maximum(peak, t)
        weights = [jnp.exp(t - peak) for t in tops]
        wp = jnp.exp(positive - peak)
        total = wp
        for k in range(4):
            total = total + stats_in[k * 2 + c, 1:2, :] * weights[k]
        loss[:, rows] = jnp.log(total) + peak - positive
        out = as_column(wp / total - 1.0, SHARE) * pos_rows[rows]
        for k in range(4):
            out = out + as_column(weights[k] / total, SHARE) * acc_in[k * 2 + c].astype(F32)
        grad[rows, :] = out

    for wait in pending:
        wait()
    wait_send(sent_ids.at[rest, pl.ds(0, 1)], sem.at[0], sem.at[1])
    wait_send(sent.at[rest, six], sem.at[2], sem.at[3])
    wait_send(back.at[rest, six], sem.at[4], sem.at[5])


def hand_out(*refs):
    copies = [pltpu.make_async_copy(refs[k], refs[4 + k], refs[8].at[k]) for k in range(4)]
    for copy in copies:
        copy.start()
    for copy in copies:
        copy.wait()


def body(features, labels, queries, bank, old_conc, neg_index):
    vmem = pl.BlockSpec(memory_space=pltpu.VMEM)
    hbm = pl.BlockSpec(memory_space=pltpu.HBM)
    outs = pl.pallas_call(
        kernel,
        out_shape=(
            jax.ShapeDtypeStruct((OWNED, HALF), F32),
            jax.ShapeDtypeStruct((1, OWNED), F32),
            jax.ShapeDtypeStruct((1, ROWS), F32),
            jax.ShapeDtypeStruct((ROWS, HALF), F32),
        ),
        in_specs=[hbm] * 6,
        out_specs=(vmem,) * 4,
        scratch_shapes=[
            pltpu.VMEM((ROWS, HALF), BF16),
            pltpu.VMEM((1, ROWS), jnp.int32),
            pltpu.VMEM((2, SHARE, HALF), BF16),
            pltpu.VMEM((OWNED, HALF), F32),
            pltpu.VMEM((1, OWNED), F32),
            pltpu.VMEM((64, 128), jnp.int32),
            pltpu.VMEM((CHIPS, 8, HALF), BF16),
            pltpu.VMEM((CHIPS, 8, 128), F32),
            pltpu.VMEM((CHIPS, 8, HALF + 128), BF16),
            pltpu.VMEM((CHIPS, 8, 128), F32),
            pltpu.VMEM((CHIPS, 8, HALF), BF16),
            pltpu.VMEM((CHIPS, 8, HALF), BF16),
            pltpu.VMEM((ROWS, OWNED), BF16),
            pltpu.VMEM((OWNED, 128), F32),
            pltpu.VMEM((8, OWNED), F32),
            pltpu.VMEM((8, OWNED), F32),
            pltpu.VMEM((OWNED, HALF), BF16),
            pltpu.VMEM((OWNED, HALF), BF16),
            pltpu.VMEM((OWNED, 128), F32),
            pltpu.VMEM((OWNED, 128), F32),
            pltpu.VMEM((2, 2, 32, HALF), BF16),
            pltpu.VMEM((2, 4, 8, 2, 32, HALF), BF16),
            pltpu.VMEM((8, SHARE, HALF), BF16),
            pltpu.VMEM((2, 2, 2 * SHARE, HALF), F32),
            pltpu.VMEM((2, 4, SHARE, HALF), BF16),
            pltpu.VMEM((8, SHARE, HALF), BF16),
            pltpu.VMEM((4, 8, SHARE), F32),
            pltpu.VMEM((8, 8, SHARE), F32),
            pltpu.VMEM((8, ROWS), F32),
            pltpu.VMEM((8, ROWS), F32),
            pltpu.SemaphoreType.DMA((96,)),
            pltpu.SemaphoreType.DMA((96,)),
            pltpu.SemaphoreType.DMA((40,)),
        ],
        compiler_params=pltpu.CompilerParams(
            collective_id=0, has_side_effects=True, vmem_limit_bytes=32 << 20
        ),
        name="step",
    )(
        *(
            pltpu.with_memory_space_constraint(a, pltpu.HBM)
            for a in (
                features,
                labels.reshape(1, ROWS),
                queries.reshape(2, SHARE, HALF),
                bank,
                old_conc.reshape(1, OWNED),
                neg_index.reshape(64, 128),
            )
        )
    )
    new_bank, new_conc, loss, grad = pl.pallas_call(
        hand_out,
        out_shape=tuple(jax.ShapeDtypeStruct(o.shape, o.dtype) for o in outs),
        in_specs=[vmem] * 4,
        out_specs=(hbm,) * 4,
        scratch_shapes=[pltpu.SemaphoreType.DMA((4,))],
        compiler_params=pltpu.CompilerParams(vmem_limit_bytes=4 << 20),
        name="hand_out",
    )(*outs)
    return new_bank, new_conc.reshape(OWNED), loss.reshape(ROWS), grad


def solution(mesh):
    return jax.shard_map(
        body,
        mesh=mesh,
        in_specs=(P("dp", "mp"), P("dp"), P("dp", "mp"), P("dp", "mp"), P("dp"), P()),
        out_specs=(P("dp", "mp"), P("dp"), P("dp"), P("dp", "mp")),
        check_vma=False,
    )
```
